256 devices in a mesh: gal: 8 (over y, core), pix: 32 (over x, z).
Axes of the slice: x: 4, y: 4, z: 8, core: 2. Of those that a mesh axis runs over, the one named last changes fastest.
Arguments:
- observed: float32 [32768, 4096], P('pix', 'gal'), may hold values from -6 to 6
- sparse_init: float32 [32768, 4096], P('pix', 'gal'), may hold values from -4 to 4
- dual_init: float32 [32768, 4096], P('pix', 'gal'), may hold values from -4 to 4
- right_init: float32 [64, 4096], P(None, 'gal'), may hold values from -0.09375 to 0.09375
Outputs:
- sparse: float32 [32768, 4096], P('pix', 'gal')
- dual: float32 [32768, 4096], P('pix', 'gal')
- left: float32 [64, 32768], P(None, 'pix')
- right: float32 [64, 4096], P(None, 'gal')
The draws below stay inside these ranges and needn't reach their ends.
All inputs are finite; a program needn't handle non-finite values.
Results may differ from the reference program's by a relative error of at most 0.0003.
Values sent between devices are 32-bit elements; how exact they have to be, the bound alone decides.
A program may use at most 64 MiB of HBM per device.

```python
import jax
import jax.numpy as jnp
from jax import lax

P_SIZE = 4096
R = 64
ITERS = 2
G = 32768


def block_scale(rng, extent, split, least, top_value):
    def one(dim, shards_of):
        draws = jax.random.uniform(jax.random.fold_in(jax.random.fold_in(rng, 6), dim), (shards_of,), jnp.float32, least / len(split), top_value / len(split))
        return jnp.repeat(jnp.exp(draws), extent[dim] // shards_of).reshape((-1,) + (1,) * (len(extent) - dim - 1))

    loudness = one(*split[0])
    for cut in split[1:]:
        loudness = loudness * one(*cut)
    return loudness


def normal_values(key, dims, spread, bound, cuts=(), held_as=jnp.bfloat16):
    level = block_scale(key, dims, cuts, -0.22, 0.18) if cuts else 1.0
    entries = jax.random.normal(key, dims, jnp.float32) * spread * level
    return jnp.minimum(jnp.maximum(entries, -bound), bound).astype(held_as)


def setup_inputs(seed: int = 0) -> dict:
    splits = jax.random.split(jax.random.key(seed), 5)
    return {
        "observed": normal_values(splits[0], (G, P_SIZE), 1.0, 6.0, ((0, 32), (1, 8)), jnp.float32),
        "sparse_init": normal_values(splits[1], (G, P_SIZE), 0.5, 4.0, ((0, 32), (1, 8)), jnp.float32),
        "dual_init": normal_values(splits[2], (G, P_SIZE), 0.5, 4.0, ((0, 32), (1, 8)), jnp.float32),
        "right_init": normal_values(splits[3], (R, P_SIZE), P_SIZE ** -0.5, 0.09375, ((1, 8),), jnp.float32),
    }


MU = 1.25
TAU = 0.6 / 1.25
HIGH = lax.Precision.HIGHEST

def orth(panel):
    gram = jnp.dot(panel, panel.T, precision=HIGH)
    factor = jnp.linalg.cholesky(gram)
    return jax.scipy.linalg.solve_triangular(factor, panel, lower=True)

def shrink(values):
    return jnp.sign(values) * jnp.maximum(jnp.abs(values) - TAU, 0.0)

def reference(observed, sparse_init, dual_init, right_init):
    sparse, dual, right = (sparse_init, dual_init, right_init)
    left = None
    for step in range(ITERS):
        target = observed - sparse + dual / MU
        panel = jnp.dot(right, target.T, precision=HIGH)
        left = orth(panel)
        wide = jnp.dot(left, target, precision=HIGH)
        lowrank = jnp.dot(left.T, wide, precision=HIGH)
        sparse = shrink(observed - lowrank + dual / MU)
        dual = dual + MU * (observed - lowrank - sparse)
        right = orth(wide)
    return (sparse, dual, left, right)
```

```python
import functools

import jax
import jax.numpy as jnp
from jax import lax
from jax.experimental import pallas as pl
from jax.experimental.pallas import tpu as pltpu
from jax.sharding import PartitionSpec as P

MU = 1.25
TAU = 0.6 / 1.25
INV_MU = 1.0 / MU
HIGH = lax.Precision.HIGHEST
MESH = pl.DeviceIdType.MESH
F32 = jnp.float32
BF16 = jnp.bfloat16

NG = 8
NZ = 8
NX = 4
R = 64
ROWS = 1024
COLS = 512
GB = ROWS // NG
RB = R // NZ
CHUNK = 256
NCH = ROWS // CHUNK

PRS, PAG, WRS, WX, WAG, KRS, KX, KAG, GAR = range(9)

NN = (((1,), (0,)), ((), ()))
NT = (((1,), (1,)), ((), ()))
TN = (((0,), (0,)), ((), ()))


def split(value):
    high = value.astype(BF16)
    return high, (value - high.astype(F32)).astype(BF16)


def mm(a, b, dims):
    return lax.dot_general(a, b, dims, preferred_element_type=F32)


def mm_high(a, b, dims):
    return lax.dot_general(a, b, dims, precision=HIGH, preferred_element_type=F32)


def inverse_factor(gram2):
    lane = lax.broadcasted_iota(jnp.int32, (8, 128), 1)
    sub = lax.broadcasted_iota(jnp.int32, (8, 128), 0)
    tiles = []
    for b in range(8):
        eye = jnp.where(lane == sub + 8 * b, 1.0, 0.0)
        tiles.append(jnp.where(lane < R, eye, gram2[8 * b : 8 * b + 8, :]))
    for j in range(R):
        t = j // 8
        pivot = tiles[t][j % 8 : j % 8 + 1, :]
        scaled = pivot * (1.0 / pivot[:, R + j : R + j + 1])
        for b in range(t, 8):
            column = tiles[b][:, R + j : R + j + 1]
            update = column * scaled
            if b == t:
                update = jnp.where(sub > j % 8, update, 0.0)
            tiles[b] = tiles[b] - update
    out = []
    for b in range(8):
        diag = jnp.sum(jnp.where(lane == sub + 8 * b + R, tiles[b], 0.0), axis=1, keepdims=True)
        out.append(tiles[b] * (1.0 / jnp.sqrt(diag)))
    return jnp.concatenate(out, axis=0)[:, :R]


def kernel(
    obs_hbm, sp_hbm, du_hbm, right_ref, x_hbm, left_ref, right_out,
    obs, work, dual, thi, tlo, lstk,
    part, prs, psrc, panel, wpart, wrs, wsrc, wx, wres, wraw,
    kpart, krs, ksrc, kx, kres, kraw, gsrc, gall,
    load_sem, store_sem, send_sem, recv_sem,
):
    g = lax.axis_index("gal")
    pix = lax.axis_index("pix")
    z = lax.rem(pix, NZ)
    x = lax.div(pix, NZ)

    def gal_peer(t):
        return {"gal": t, "pix": pix}

    def z_peer(t):
        return {"gal": g, "pix": x * NZ + t}

    def x_peer(t):
        return {"gal": g, "pix": t * NZ + z}

    def loads(ch):
        rows = pl.ds(ch * CHUNK, CHUNK)
        return [
            pltpu.make_async_copy(src.at[rows, :], dst.at[rows, :], load_sem.at[i, ch])
            for i, (src, dst) in enumerate(((obs_hbm, obs), (sp_hbm, work), (du_hbm, dual)))
        ]

    barrier = pltpu.get_barrier_semaphore()
    for n, me, peer in ((NG, g, gal_peer), (NZ, z, z_peer), (NX, x, x_peer)):
        for k in range(1, n):
            pl.semaphore_signal(barrier, inc=1, device_id=peer(lax.rem(me + k, n)), device_id_type=MESH)
    for ch in range(NCH):
        for copy in loads(ch):
            copy.start()

    def send(it, kind, src, dst, peer):
        pltpu.make_async_remote_copy(
            src_ref=src, dst_ref=dst, send_sem=send_sem.at[it, kind], recv_sem=recv_sem.at[it, kind],
            device_id=peer, device_id_type=MESH,
        ).start()

    def spread(it, kind, n, me, peer, src_of, dst):
        order = sorted(range(1, n), key=lambda k: -min(k, n - k))
        for k in order:
            t = lax.rem(me + k, n)
            send(it, kind, src_of(t), dst.at[it, me], peer(t))

    def arrived(it, kind, n, dst):
        view = dst.at[it, pl.ds(0, n - 1)]
        pltpu.make_async_copy(view, view, recv_sem.at[it, kind]).wait()

    def sent(it, kind, n, dst):
        view = dst.at[it, pl.ds(0, n - 1)]
        pltpu.make_async_copy(view, view, send_sem.at[it, kind]).wait()

    def total(buf, it, n):
        acc = buf[it, 0]
        for i in range(1, n):
            acc = acc + buf[it, i]
        return acc

    def panel_chunk(it, ch, r2, r_high, t_high, t_low):
        both = mm(r2, t_high, NT)
        p = both[:R] + both[R:] + mm(r_high, t_low, NT)
        for i in range(CHUNK // GB):
            d = ch * (CHUNK // GB) + i
            part[it, d] = p[:, i * GB : (i + 1) * GB]

            @pl.when(g != d)
            def _():
                send(it, PRS, part.at[it, d], prs.at[it, g], gal_peer(d))

    def finish_panel(it):
        prs[it, g] = part[it, g]

    r_high, r_low = split(right_ref[...])
    r2 = jnp.concatenate([r_high, r_low], axis=0)
    for ch in range(NCH):
        rows = pl.ds(ch * CHUNK, CHUNK)
        for copy in loads(ch):
            copy.wait()
        c = dual[rows, :] * INV_MU
        dual[rows, :] = c
        t_high, t_low = split(obs[rows, :] - work[rows, :] + c)
        thi[rows, :] = t_high
        tlo[rows, :] = t_low
        if ch == 0:
            pl.semaphore_wait(barrier, NG + NZ + NX - 3)
        panel_chunk(0, ch, r2, r_high, t_high, t_low)
    finish_panel(0)

    inv_right = None
    for it in range(2):
        if it == 1:
            arrived(0, GAR, NG, gall)
            packed = total(gall, 0, NG)
            inv_right = inverse_factor(jnp.concatenate([pltpu.roll(packed, R, 1), packed], axis=0))
        arrived(it, PRS, NG, prs)
        mine = total(prs, it, NG)
        if it == 1:
            mine = mm_high(inv_right, mine, NN)
        psrc[it] = mine
        spread(it, PAG, NG, g, gal_peer, lambda t: psrc.at[it], panel)
        panel[it, g] = mine
        arrived(it, PAG, NG, panel)
        whole = jnp.concatenate([panel[it, i] for i in range(NG)], axis=1)

        gram = mm_high(whole, jnp.concatenate([whole, whole], axis=0), NT)
        for d in range(NZ):
            kpart[it, d] = gram[d * RB : (d + 1) * RB]
        spread(it, KRS, NZ, z, z_peer, lambda t: kpart.at[it, t], krs)
        krs[it, z] = kpart[it, z]

        p_high, p_low = split(whole)
        p2 = jnp.concatenate([p_high, p_low], axis=0)
        both = mm(p2, thi[...], NN)
        raw = both[:R] + both[R:] + mm(p_high, tlo[...], NN)
        for d in range(NZ):
            wpart[it, d] = raw[d * RB : (d + 1) * RB]
        spread(it, WRS, NZ, z, z_peer, lambda t: wpart.at[it, t], wrs)
        wrs[it, z] = wpart[it, z]

        arrived(it, KRS, NZ, krs)
        mine = total(krs, it, NZ)
        ksrc[it] = mine
        spread(it, KX, NX, x, x_peer, lambda t: ksrc.at[it], kx)
        kx[it, x] = mine
        arrived(it, KX, NX, kx)
        mine = total(kx, it, NX)
        kres[it] = mine
        spread(it, KAG, NZ, z, z_peer, lambda t: kres.at[it], kraw)
        kraw[it, z] = mine

        arrived(it, WRS, NZ, wrs)
        mine = total(wrs, it, NZ)
        wsrc[it] = mine
        spread(it, WX, NX, x, x_peer, lambda t: wsrc.at[it], wx)
        wx[it, x] = mine
        arrived(it, WX, NX, wx)
        mine = total(wx, it, NX)
        wres[it] = mine
        spread(it, WAG, NZ, z, z_peer, lambda t: wres.at[it], wraw)
        wraw[it, z] = mine

        arrived(it, KAG, NZ, kraw)
        inv_left = inverse_factor(jnp.concatenate([kraw[it, i] for i in range(NZ)], axis=0))
        left = mm_high(inv_left, whole, NN)
        l_high, l_low = split(left)
        lstk[0:R, :] = l_high
        lstk[R : 2 * R, :] = l_high
        lstk[2 * R : 3 * R, :] = l_low
        if it == 1:
            left_ref[...] = left

        arrived(it, WAG, NZ, wraw)
        wide = mm_high(inv_left, jnp.concatenate([wraw[it, i] for i in range(NZ)], axis=0), NN)
        w_high, w_low = split(wide)
        wstk = jnp.concatenate([w_high, w_low, w_high], axis=0)

        gram = mm_high(wide, jnp.concatenate([wide, wide], axis=0), NT)
        lane = lax.broadcasted_iota(jnp.int32, (R // 2, 128), 1)
        packed = jnp.where(lane < R, gram[: R // 2], gram[R // 2 :])
        gsrc[it] = packed
        spread(it, GAR, NG, g, gal_peer, lambda t: gsrc.at[it], gall)
        gall[it, g] = packed

        r2 = jnp.concatenate([w_high, w_low], axis=0)
        for ch in range(NCH):
            rows = pl.ds(ch * CHUNK, CHUNK)
            low = mm(lstk[:, rows], wstk, TN)
            c = dual[rows, :]
            v = obs[rows, :] + c - low
            if it == 0:
                clipped = jnp.minimum(jnp.maximum(v, -TAU), TAU)
                dual[rows, :] = clipped
                t_high, t_low = split(low - c + (clipped + clipped))
                thi[rows, :] = t_high
                tlo[rows, :] = t_low
                panel_chunk(1, ch, r2, w_high, t_high, t_low)
            else:
                work[rows, :] = v
                pltpu.make_async_copy(work.at[rows, :], x_hbm.at[rows, :], store_sem.at[ch]).start()
        if it == 0:
            finish_panel(1)
        else:
            arrived(1, GAR, NG, gall)
            packed = total(gall, 1, NG)
            inv_right = inverse_factor(jnp.concatenate([pltpu.roll(packed, R, 1), packed], axis=0))
            right_out[...] = mm_high(inv_right, wide, NN)

    for ch in range(NCH):
        rows = pl.ds(ch * CHUNK, CHUNK)
        pltpu.make_async_copy(work.at[rows, :], x_hbm.at[rows, :], store_sem.at[ch]).wait()
    for it in range(2):
        for kind, n, buf in (
            (PRS, NG, prs), (PAG, NG, panel), (WRS, NZ, wrs), (WX, NX, wx), (WAG, NZ, wraw),
            (KRS, NZ, krs), (KX, NX, kx), (KAG, NZ, kraw), (GAR, NG, gall),
        ):
            sent(it, kind, n, buf)


def per_device(observed, sparse_init, dual_init, right_init):
    hbm = pl.BlockSpec(memory_space=pl.ANY)
    vmem = pl.BlockSpec(memory_space=pltpu.VMEM)
    shape = (ROWS, COLS)
    x, left, right = pl.pallas_call(
        kernel,
        out_shape=(
            jax.ShapeDtypeStruct(shape, F32),
            jax.ShapeDtypeStruct((R, ROWS), F32),
            jax.ShapeDtypeStruct((R, COLS), F32),
        ),
        in_specs=[hbm, hbm, hbm, vmem],
        out_specs=(hbm, vmem, vmem),
        scratch_shapes=[
            pltpu.VMEM(shape, F32),
            pltpu.VMEM(shape, F32),
            pltpu.VMEM(shape, F32),
            pltpu.VMEM(shape, BF16),
            pltpu.VMEM(shape, BF16),
            pltpu.VMEM((3 * R, ROWS), BF16),
            pltpu.VMEM((2, NG, R, GB), F32),
            pltpu.VMEM((2, NG, R, GB), F32),
            pltpu.VMEM((2, R, GB), F32),
            pltpu.VMEM((2, NG, R, GB), F32),
            pltpu.VMEM((2, NZ, RB, COLS), F32),
            pltpu.VMEM((2, NZ, RB, COLS), F32),
            pltpu.VMEM((2, RB, COLS), F32),
            pltpu.VMEM((2, NX, RB, COLS), F32),
            pltpu.VMEM((2, RB, COLS), F32),
            pltpu.VMEM((2, NZ, RB, COLS), F32),
            pltpu.VMEM((2, NZ, RB, 2 * R), F32),
            pltpu.VMEM((2, NZ, RB, 2 * R), F32),
            pltpu.VMEM((2, RB, 2 * R), F32),
            pltpu.VMEM((2, NX, RB, 2 * R), F32),
            pltpu.VMEM((2, RB, 2 * R), F32),
            pltpu.VMEM((2, NZ, RB, 2 * R), F32),
            pltpu.VMEM((2, R // 2, 2 * R), F32),
            pltpu.VMEM((2, NG, R // 2, 2 * R), F32),
            pltpu.SemaphoreType.DMA((3, NCH)),
            pltpu.SemaphoreType.DMA((NCH,)),
            pltpu.SemaphoreType.DMA((2, 9)),
            pltpu.SemaphoreType.DMA((2, 9)),
        ],
        compiler_params=pltpu.CompilerParams(collective_id=0, has_side_effects=True, vmem_limit_bytes=48 << 20),
        name="pursuit",
    )(observed, sparse_init, dual_init, right_init)
    clipped = jnp.minimum(jnp.maximum(x, -TAU), TAU)
    return x - clipped, MU * clipped, left, right


def solution(mesh):
    return jax.shard_map(
        per_device,
        mesh=mesh,
        in_specs=(P("pix", "gal"), P("pix", "gal"), P("pix", "gal"), P(None, "gal")),
        out_specs=(P("pix", "gal"), P("pix", "gal"), P(None, "pix"), P(None, "gal")),
        check_vma=False,
    )
```

```python
import contextlib

import jax
import jax.numpy as jnp
from jax import lax
from jax.experimental import pallas as pl
from jax.experimental.pallas import tpu as pltpu
from jax.sharding import PartitionSpec as P

MU = 1.25
TAU = 0.6 / 1.25
INV_MU = 1.0 / MU
HIGH = lax.Precision.HIGHEST
MESH = pl.DeviceIdType.MESH
F32 = jnp.float32
BF16 = jnp.bfloat16

NY = 4
NG = 8
NZ = 8
NX = 4
NP = NZ * NX
R = 64
ROWS = 1024
COLS = 512
GB = ROWS // NG
RB = 8
LB = 128
CHUNK = ROWS // NY
ORDER = (2, 1, 3, 0)

PIX_ORDER = sorted(
    ((i, j) for i in range(NX) for j in range(NZ) if i or j), key=lambda k: -(min(k[0], NX - k[0]) + min(k[1], NZ - k[1]))
)

PRS, PAG, WRS, WAG, KZ, KX, KAG, GAR = range(8)

NN = (((1,), (0,)), ((), ()))
NT = (((1,), (1,)), ((), ()))
TN = (((0,), (0,)), ((), ()))


def split(value):
    high = value.astype(BF16)
    return high, (value - high.astype(F32)).astype(BF16)


def mm(a, b, dims):
    return lax.dot_general(a, b, dims, preferred_element_type=F32)


def mm_high(a, b, dims):
    return lax.dot_general(a, b, dims, precision=HIGH, preferred_element_type=F32)


def clip(value):
    return jnp.minimum(jnp.maximum(value, -TAU), TAU)


def inverse_factor(gram2):
    tile = (8, 128)
    lane = lax.broadcasted_iota(jnp.int32, tile, 1)
    sub = lax.broadcasted_iota(jnp.int32, tile, 0)
    tiles, out = [], []
    for b in range(8):
        eye = jnp.where(lane == sub + 8 * b, 1.0, 0.0)
        tiles.append(jnp.where(lane < R, eye, gram2[8 * b : 8 * b + 8, :]))
        out.append(None)

    def column(value, k):
        return jnp.broadcast_to(value[:, R + k : R + k + 1], tile)

    for j in range(0, R, 4):
        t, o = j // 8, j % 8
        r0, r1, r2, r3 = (jnp.broadcast_to(tiles[t][o + p : o + p + 1, :], tile) for p in range(4))
        a00, a01, b00, b01 = (column(r0, j + q) for q in range(4))
        a11, b10, b11 = (column(r1, j + q) for q in range(1, 4))
        d00, d01 = (column(r2, j + q) for q in range(2, 4))
        d11 = column(r3, j + 3)
        det = a00 * a11 - a01 * a01
        inv = 1.0 / det
        n00, n01, n11 = a11 * inv, -(a01 * inv), a00 * inv
        x00, x01 = n00 * b00 + n01 * b10, n00 * b01 + n01 * b11
        x10, x11 = n01 * b00 + n11 * b10, n01 * b01 + n11 * b11
        s00 = d00 - (b00 * x00 + b10 * x10)
        s01 = d01 - (b00 * x01 + b10 * x11)
        s11 = d11 - (b01 * x01 + b11 * x11)
        sdet = s00 * s11 - s01 * s01
        sinv = 1.0 / sdet
        m00, m01, m11 = s11 * sinv, -(s01 * sinv), s00 * sinv
        u2 = r2 - (x00 * r0 + x10 * r1)
        u3 = r3 - (x01 * r0 + x11 * r1)
        if j + 4 < R:
            y2, y3 = m00 * u2 + m01 * u3, m01 * u2 + m11 * u3
            y0 = (n00 * r0 + n01 * r1) - (x00 * y2 + x01 * y3)
            y1 = (n01 * r0 + n11 * r1) - (x10 * y2 + x11 * y3)
            for b in range(t if o == 0 else t + 1, 8):
                c0, c1, c2, c3 = (column(tiles[b], j + p) for p in range(4))
                update = (c0 * y0 + c1 * y1) + (c2 * y2 + c3 * y3)
                if b == t:
                    update = jnp.where(sub >= 4, update, 0.0)
                tiles[b] = tiles[b] - update
        f0 = r0 * (1.0 / jnp.sqrt(a00))
        f1 = (r1 - (a01 / a00) * r0) * (1.0 / jnp.sqrt(det / a00))
        f2 = u2 * (1.0 / jnp.sqrt(s00))
        f3 = (u3 - (s01 / s00) * u2) * (1.0 / jnp.sqrt(sdet / s00))
        quad = jnp.where(sub == o, f0, jnp.where(sub == o + 1, f1, jnp.where(sub == o + 2, f2, f3)))
        out[t] = quad if o == 0 else jnp.where(sub < 4, out[t], quad)
    return jnp.concatenate(out, axis=0)[:, :R]


def factor_of(packed):
    return inverse_factor(jnp.concatenate([pltpu.roll(packed, R, 1), packed], axis=0))


def scope(name):
    return contextlib.nullcontext()


def kernel(
    obs_hbm, sp_hbm, du_hbm, right_hbm, sparse_out, dual_out, left_ref, wide_ref, gram_ref,
    right_ref, obs, work, dual, thi, tlo, lstk,
    part, prs, panel, normal, wpart, wrs, wraw, kz, kx, kraw, gall,
    load_sem, send_sem, recv_sem, near_sem, relay_sem,
):
    g = lax.axis_index("gal")
    pix = lax.axis_index("pix")
    y, core = lax.div(g, 2), lax.rem(g, 2)
    other = 1 - core
    z = lax.rem(pix, NZ)
    x = lax.div(pix, NZ)

    def gal_peer(t):
        return {"gal": t, "pix": pix}

    def z_peer(t):
        return {"gal": g, "pix": x * NZ + t}

    def x_peer(t):
        return {"gal": g, "pix": t * NZ + z}

    def pix_of(k):
        return lax.rem(x + k[0], NX) * NZ + lax.rem(z + k[1], NZ)

    def pix_peer(k):
        return {"gal": g, "pix": pix_of(k)}

    def chunk(k):
        return lax.rem(y + k, NY)

    def rows_of(k):
        return pl.ds(pl.multiple_of(chunk(k) * CHUNK, CHUNK), CHUNK)

    def loads(k):
        rows = rows_of(k)
        return [
            pltpu.make_async_copy(src.at[rows, :], dst.at[rows, :], load_sem.at[i, k])
            for i, (src, dst) in enumerate(((obs_hbm, obs), (sp_hbm, work), (du_hbm, dual)))
        ]

    barrier = pltpu.get_barrier_semaphore()
    for k in PIX_ORDER:
        pl.semaphore_signal(barrier, inc=1, device_id=pix_peer(k), device_id_type=MESH)
    for k in range(1, NG):
        pl.semaphore_signal(barrier, inc=1, device_id=gal_peer(lax.rem(g + k, NG)), device_id_type=MESH)
    load_right = pltpu.make_async_copy(right_hbm, right_ref, load_sem.at[3, 0])
    load_right.start()
    for k in ORDER:
        for copy in loads(k):
            copy.start()

    def send(it, kind, src, dst, peer, recv):
        pltpu.make_async_remote_copy(
            src_ref=src, dst_ref=dst, send_sem=send_sem.at[it, kind], recv_sem=recv,
            device_id=peer, device_id_type=MESH,
        ).start()

    def spread(it, kind, n, me, peer, src_of, dst):
        order = sorted(range(1, n), key=lambda k: -min(k, n - k))
        for k in order:
            t = lax.rem(me + k, n)
            send(it, kind, src_of(t), dst.at[it, me], peer(t), recv_sem.at[it, kind])

    def arrived(it, kind, n, dst):
        view = dst.at[it, pl.ds(0, n - 1)]
        pltpu.make_async_copy(view, view, recv_sem.at[it, kind]).wait()

    def landed(view, sem):
        pltpu.make_async_copy(view, view, sem).wait()

    def total(buf, it, n):
        acc = buf[it, 0]
        for i in range(1, n):
            acc = acc + buf[it, i]
        return acc

    def panel_chunk(it, k, r2, r_high, t_high, t_low):
        both = mm(r2, t_high, NT)
        p = both[:R] + both[R:] + mm(r_high, t_low, NT)
        first = 2 * chunk(k)
        part[it, first] = p[:, :GB]
        part[it, first + 1] = p[:, GB:]

    def send_chunk(it, k):
        first = 2 * chunk(k)
        if k == 0:
            send(it, PRS, part.at[it, 2 * y + other], prs.at[it, g], gal_peer(2 * y + other), recv_sem.at[it, PRS])
            prs[it, g] = part[it, g]
        else:
            for d in (first, first + 1):
                send(it, PRS, part.at[it, d], prs.at[it, g], gal_peer(d), recv_sem.at[it, PRS])

    with scope("load_right"):
        load_right.wait()
        r_high, r_low = split(right_ref[...])
        r2 = jnp.concatenate([r_high, r_low], axis=0)
    for k in ORDER:
        with scope("load"):
            for copy in loads(k):
                copy.wait()
        with scope("target"):
            rows = rows_of(k)
            c = dual[rows, :] * INV_MU
            dual[rows, :] = c
            t_high, t_low = split(obs[rows, :] - work[rows, :] + c)
            thi[rows, :] = t_high
            tlo[rows, :] = t_low
        with scope("panel"):
            panel_chunk(0, k, r2, r_high, t_high, t_low)
    with scope("barrier"):
        pl.semaphore_wait(barrier, NG + NP - 2)
    for k in ORDER:
        send_chunk(0, k)

    for it in range(2):
        with scope("w_prs"):
            arrived(it, PRS, NG, prs)
        with scope("pag_send"):
            panel[it, g] = total(prs, it, NG)
            own = panel.at[it, g]
            for k in (2, 1, 3):
                send(it, PAG, own, own, gal_peer(2 * chunk(k) + core), near_sem.at[it, NY - k])
            partner = gal_peer(2 * y + other)
            send(it, PAG, own, own, partner, near_sem.at[it, 0])
        if it == 1:
            with scope("w_gar"):
                arrived(0, GAR, NG, gall)
            with scope("chol_right"):
                inv_right = factor_of(total(gall, 0, NG))

        gram = raw = None
        for k in (0, 1, 3, 2):
            block = 2 * chunk(k)
            rows = rows_of(k)
            with scope("w_near"):
                landed(panel.at[it, block + other], near_sem.at[it, 0] if k == 0 else relay_sem.at[it, k])
            with scope("gram_left"):
                p = jnp.concatenate([panel[it, block], panel[it, block + 1]], axis=1)
                if it == 1:
                    p = mm_high(inv_right, p, NN)
                normal[:, rows] = p
                few = normal[pl.ds(pl.multiple_of(g * RB, RB), RB), rows]
                term = mm_high(few, jnp.concatenate([p, p], axis=0), NT)
                gram = term if gram is None else gram + term
                if k == 2:
                    kz[it, z] = gram
                    spread(it, KZ, NZ, z, z_peer, lambda t: kz.at[it, z], kz)
            with scope("raw_wide"):
                p_high, p_low = split(p)
                both = mm(jnp.concatenate([p_high, p_low], axis=0), thi[rows, :], NN)
                term = both[:R] + both[R:] + mm(p_high, tlo[rows, :], NN)
                raw = term if raw is None else raw + term
            if k == 0:
                with scope("w_relay"):
                    for kk in (1, 3, 2):
                        slot = panel.at[it, 2 * chunk(kk) + core]
                        landed(slot, near_sem.at[it, kk])
                        send(it, PAG, slot, slot, partner, relay_sem.at[it, kk])
        with scope("w_send"):
            for i in range(NX):
                for j in range(NZ):
                    wpart[it, i * NZ + j] = raw[j * RB : (j + 1) * RB, i * LB : (i + 1) * LB]
            for k in PIX_ORDER:
                send(it, WRS, wpart.at[it, pix_of(k)], wrs.at[it, pix], pix_peer(k), recv_sem.at[it, WRS])
            wrs[it, pix] = wpart[it, pix]

        with scope("w_kz"):
            arrived(it, KZ, NZ, kz)
        kx[it, x] = total(kz, it, NZ)
        spread(it, KX, NX, x, x_peer, lambda t: kx.at[it, x], kx)
        with scope("w_wrs"):
            arrived(it, WRS, NP, wrs)
        with scope("wag_send"):
            wraw[it, pix] = total(wrs, it, NP)
            own = wraw.at[it, pix]
            for k in PIX_ORDER:
                send(it, WAG, own, own, pix_peer(k), recv_sem.at[it, WAG])
        with scope("w_kx"):
            arrived(it, KX, NX, kx)
        kraw[it, g] = total(kx, it, NX)
        spread(it, KAG, NG, g, gal_peer, lambda t: kraw.at[it, g], kraw)

        with scope("w_kag"):
            arrived(it, KAG, NG, kraw)
        with scope("chol_left"):
            inv_left = inverse_factor(jnp.concatenate([kraw[it, i] for i in range(NG)], axis=0))
        with scope("left"):
            left = mm_high(inv_left, normal[...], NN)
            l_high, l_low = split(left)
            lstk[0:R, :] = l_high
            lstk[R : 2 * R, :] = l_high
            lstk[2 * R : 3 * R, :] = l_low
            if it == 1:
                left_ref[...] = left

        with scope("w_wag"):
            arrived(it, WAG, NP, wraw)
        with scope("wide"):
            columns = [jnp.concatenate([wraw[it, i * NZ + j] for j in range(NZ)], axis=0) for i in range(NX)]
            wide = mm_high(inv_left, jnp.concatenate(columns, axis=1), NN)
            w_high, w_low = split(wide)
            wstk = jnp.concatenate([w_high, w_low, w_high], axis=0)
            r2 = jnp.concatenate([w_high, w_low], axis=0)
        with scope("gram_right"):
            gram = mm_high(wide, jnp.concatenate([wide, wide], axis=0), NT)
            lane = lax.broadcasted_iota(jnp.int32, (R // 2, 128), 1)
            gall[it, g] = jnp.where(lane < R, gram[: R // 2], gram[R // 2 :])
            spread(it, GAR, NG, g, gal_peer, lambda t: gall.at[it, g], gall)
        for k in ORDER:
            with scope("update"):
                rows = rows_of(k)
                low = mm(lstk[:, rows], wstk, TN)
                c = dual[rows, :]
                if it == 0:
                    clipped = clip(obs[rows, :] + c - low)
                    dual[rows, :] = clipped
                    t_high, t_low = split(low - c + (clipped + clipped))
                    thi[rows, :] = t_high
                    tlo[rows, :] = t_low
                    panel_chunk(1, k, r2, w_high, t_high, t_low)
                    send_chunk(1, k)
                else:
                    v = obs[rows, :] + c - low
                    clipped = clip(v)
                    sparse_out[rows, :] = v - clipped
                    dual_out[rows, :] = MU * clipped

    wide_ref[...] = wide
    with scope("w_gar"):
        arrived(1, GAR, NG, gall)
    gram_ref[...] = total(gall, 1, NG)
    with scope("fin"):
        for it in range(2):
            for kind, n, buf in (
                (PRS, NG, prs), (PAG, NG, panel), (WRS, NP, wrs), (WAG, NP, wraw),
                (KZ, NZ, kz), (KX, NX, kx), (KAG, NG, kraw), (GAR, NG, gall),
            ):
                landed(buf.at[it, pl.ds(0, n - 1)], send_sem.at[it, kind])


def outputs(
    sparse, dual, left, wide, gram, sparse_hbm, dual_hbm, left_hbm, right_hbm, right, sem,
):
    copies = [
        pltpu.make_async_copy(src, dst, sem.at[i])
        for i, (src, dst) in enumerate(((sparse, sparse_hbm), (dual, dual_hbm), (left, left_hbm), (right, right_hbm)))
    ]
    for copy in copies[:3]:
        copy.start()
    right[...] = mm_high(factor_of(gram[...]), wide[...], NN)
    copies[3].start()
    for copy in copies:
        copy.wait()


def per_device(observed, sparse_init, dual_init, right_init):
    hbm = pl.BlockSpec(memory_space=pltpu.HBM)
    vmem = pl.BlockSpec(memory_space=pltpu.VMEM)
    shape = (ROWS, COLS)
    whole = jax.ShapeDtypeStruct(shape, F32)
    left_shape = jax.ShapeDtypeStruct((R, ROWS), F32)
    right_shape = jax.ShapeDtypeStruct((R, COLS), F32)
    state = pl.pallas_call(
        kernel,
        out_shape=(whole, whole, left_shape, right_shape, jax.ShapeDtypeStruct((R // 2, 2 * R), F32)),
        in_specs=[hbm] * 4,
        out_specs=(vmem,) * 5,
        scratch_shapes=[
            pltpu.VMEM((R, COLS), F32),
            pltpu.VMEM(shape, F32),
            pltpu.VMEM(shape, F32),
            pltpu.VMEM(shape, F32),
            pltpu.VMEM(shape, BF16),
            pltpu.VMEM(shape, BF16),
            pltpu.VMEM((3 * R, ROWS), BF16),
            pltpu.VMEM((2, NG, R, GB), F32),
            pltpu.VMEM((2, NG, R, GB), F32),
            pltpu.VMEM((2, NG, R, GB), F32),
            pltpu.VMEM((R, ROWS), F32),
            pltpu.VMEM((2, NP, RB, LB), F32),
            pltpu.VMEM((2, NP, RB, LB), F32),
            pltpu.VMEM((2, NP, RB, LB), F32),
            pltpu.VMEM((2, NZ, RB, 2 * R), F32),
            pltpu.VMEM((2, NX, RB, 2 * R), F32),
            pltpu.VMEM((2, NG, RB, 2 * R), F32),
            pltpu.VMEM((2, NG, R // 2, 2 * R), F32),
            pltpu.SemaphoreType.DMA((4, NY)),
            pltpu.SemaphoreType.DMA((2, 8)),
            pltpu.SemaphoreType.DMA((2, 8)),
            pltpu.SemaphoreType.DMA((2, NY)),
            pltpu.SemaphoreType.DMA((2, NY)),
        ],
        compiler_params=pltpu.CompilerParams(collective_id=0, has_side_effects=True, vmem_limit_bytes=48 << 20),
        name="pursuit",
    )(*(pltpu.with_memory_space_constraint(a, pltpu.HBM) for a in (observed, sparse_init, dual_init, right_init)))
    return pl.pallas_call(
        outputs,
        out_shape=(whole, whole, left_shape, right_shape),
        in_specs=[vmem] * 5,
        out_specs=(hbm,) * 4,
        scratch_shapes=[
            pltpu.VMEM((R, COLS), F32),
            pltpu.SemaphoreType.DMA((4,)),
        ],
        compiler_params=pltpu.CompilerParams(vmem_limit_bytes=24 << 20),
        name="outputs",
    )(*state)


def solution(mesh):
    return jax.shard_map(
        per_device,
        mesh=mesh,
        in_specs=(P("pix", "gal"), P("pix", "gal"), P("pix", "gal"), P(None, "gal")),
        out_specs=(P("pix", "gal"), P("pix", "gal"), P(None, "pix"), P(None, "gal")),
        check_vma=False,
    )
```

```python
import contextlib

import jax
import jax.numpy as jnp
from jax import lax
from jax.experimental import pallas as pl
from jax.experimental.pallas import tpu as pltpu
from jax.sharding import PartitionSpec as P

MU = 1.25
TAU = 0.6 / 1.25
INV_MU = 1.0 / MU
HIGH = lax.Precision.HIGHEST
MESH = pl.DeviceIdType.MESH
F32 = jnp.float32
BF16 = jnp.bfloat16

NY = 4
NG = 8
NZ = 8
NX = 4
NP = NZ * NX
R = 64
ROWS = 1024
COLS = 512
GB = ROWS // NG
RB = 8
LB = 128
CHUNK = ROWS // NY
ORDER = (2, 1, 3, 0)

PIX_ORDER = sorted(
    ((i, j) for i in range(NX) for j in range(NZ) if i or j), key=lambda k: -(min(k[0], NX - k[0]) + min(k[1], NZ - k[1]))
)

PEX, PRS, PAG, WRS, WAG, KG, KZ, KX, KAG, GAR = range(10)

NN = (((1,), (0,)), ((), ()))
NT = (((1,), (1,)), ((), ()))
TN = (((0,), (0,)), ((), ()))


def split(value):
    high = value.astype(BF16)
    return high, (value - high.astype(F32)).astype(BF16)


def split3(value):
    high = value.astype(BF16)
    mid, low = split(value - high.astype(F32))
    return high, mid, low


def mm(a, b, dims):
    return lax.dot_general(a, b, dims, preferred_element_type=F32)


def mm_high(a, b, dims):
    return lax.dot_general(a, b, dims, precision=HIGH, preferred_element_type=F32)


def twin_gram(value):
    high, mid, low = split3(value)
    out = mm(jnp.concatenate([high, mid, low], axis=0), jnp.concatenate([high, high, mid, mid, low, low], axis=0), NT)
    out = out[:R] + (out[R : 2 * R] + out[2 * R :])
    return out[:, : 2 * R] + (out[:, 2 * R : 4 * R] + out[:, 4 * R :])


def stacked(value):
    return jnp.concatenate(split3(value), axis=0)


def mm3(a, high, mid, low, dims):
    first = mm(a, high, dims)
    second = mm(a[: 2 * R], mid, dims)
    third = mm(a[:R], low, dims)
    return first[:R] + ((first[R : 2 * R] + second[:R]) + (first[2 * R :] + second[R:] + third))


def clip(value):
    return jnp.minimum(jnp.maximum(value, -TAU), TAU)


def solver(e00, e01, e02, e03, e11, e12, e13, e22, e23, e33):
    det = e00 * e11 - e01 * e01
    inv = 1.0 / det
    n00, n01, n11 = e11 * inv, -(e01 * inv), e00 * inv
    x00, x01 = n00 * e02 + n01 * e12, n00 * e03 + n01 * e13
    x10, x11 = n01 * e02 + n11 * e12, n01 * e03 + n11 * e13
    s00 = e22 - (e02 * x00 + e12 * x10)
    s01 = e23 - (e02 * x01 + e12 * x11)
    s11 = e33 - (e03 * x01 + e13 * x11)
    sdet = s00 * s11 - s01 * s01
    sinv = 1.0 / sdet
    m00, m01, m11 = s11 * sinv, -(s01 * sinv), s00 * sinv

    def reduce(v0, v1, v2, v3):
        return v2 - (x00 * v0 + x10 * v1), v3 - (x01 * v0 + x11 * v1)

    def solve(v0, v1, v2, v3):
        u2, u3 = reduce(v0, v1, v2, v3)
        y2, y3 = m00 * u2 + m01 * u3, m01 * u2 + m11 * u3
        y0 = (n00 * v0 + n01 * v1) - (x00 * y2 + x01 * y3)
        y1 = (n01 * v0 + n11 * v1) - (x10 * y2 + x11 * y3)
        return y0, y1, y2, y3

    def factor(v0, v1, v2, v3):
        u2, u3 = reduce(v0, v1, v2, v3)
        return (
            v0 * (1.0 / jnp.sqrt(e00)),
            (v1 - (e01 / e00) * v0) * (1.0 / jnp.sqrt(det / e00)),
            u2 * (1.0 / jnp.sqrt(s00)),
            (u3 - (s01 / s00) * u2) * (1.0 / jnp.sqrt(sdet / s00)),
        )

    return solve, factor


def inverse_factor(gram2):
    tile = (8, 128)
    lane = lax.broadcasted_iota(jnp.int32, tile, 1)
    sub = lax.broadcasted_iota(jnp.int32, tile, 0)
    tiles, out = [], []
    for b in range(8):
        eye = jnp.where(lane == sub + 8 * b, 1.0, 0.0)
        tiles.append(jnp.where(lane < R, eye, gram2[8 * b : 8 * b + 8, :]))

    def row(value, p):
        return jnp.broadcast_to(value[p : p + 1, :], tile)

    def four(e, first):
        return [e[first + p, first + q] for p in range(4) for q in range(p, 4)]

    for t in range(8):
        columns = [
            [jnp.broadcast_to(tiles[b][:, R + 8 * t + q : R + 8 * t + q + 1], tile) for q in range(8)] for b in range(t, 8)
        ]
        rows = [row(tiles[t], p) for p in range(8)]
        e = {(p, q): row(columns[0][q], p) for q in range(8) for p in range(q + 1)}
        solve, factor = solver(*four(e, 0))
        upper = rows[:4]
        y = solve(*upper)
        cross = [solve(*(e[r, q] for r in range(4))) for q in range(4, 8)]

        def less(value, p, ys):
            return value - ((e[0, p] * ys[0] + e[1, p] * ys[1]) + (e[2, p] * ys[2] + e[3, p] * ys[3]))

        late = {(p, q): less(e[p, q], p, cross[q - 4]) for q in range(4, 8) for p in range(4, q + 1)}
        lower = [less(rows[p], p, y) for p in range(4, 8)]
        solve_late, factor_late = solver(*four(late, 4))
        done = [*factor(*upper), *factor_late(*lower)]
        result = done[7]
        for p in range(6, -1, -1):
            result = jnp.where(sub == p, done[p], result)
        out.append(result)
        if t < 7:
            w = solve_late(*lower)
            full = [
                y[r] - ((cross[0][r] * w[0] + cross[1][r] * w[1]) + (cross[2][r] * w[2] + cross[3][r] * w[3]))
                for r in range(4)
            ] + list(w)
            for b in range(t + 1, 8):
                terms = [columns[b - t][q] * full[q] for q in range(8)]
                tiles[b] = tiles[b] - (
                    ((terms[0] + terms[1]) + (terms[2] + terms[3])) + ((terms[4] + terms[5]) + (terms[6] + terms[7]))
                )
    return jnp.concatenate(out, axis=0)


def product(inverse, value):
    return mm_high(inverse[:, :R], value, NN)


def factor_of(packed):
    return inverse_factor(jnp.concatenate([pltpu.roll(packed, R, 1), packed], axis=0))


def scope(name):
    return contextlib.nullcontext()


def kernel(
    obs_hbm, sp_hbm, du_hbm, right_hbm, sparse_out, dual_out, left_ref, wide_ref, gram_ref,
    right_ref, obs, work, dual, thi, tmid, tlo, lstk,
    part, pex, prs, panel, normal, wpart, wrs, wraw, kpart, kg, kz, kx, kraw, gall,
    load_sem, send_sem, recv_sem, pex_sem, near_sem, relay_sem,
):
    g = lax.axis_index("gal")
    pix = lax.axis_index("pix")
    y, core = lax.div(g, 2), lax.rem(g, 2)
    other = 1 - core
    z = lax.rem(pix, NZ)
    x = lax.div(pix, NZ)

    def gal_peer(t):
        return {"gal": t, "pix": pix}

    def z_peer(t):
        return {"gal": g, "pix": x * NZ + t}

    def x_peer(t):
        return {"gal": g, "pix": t * NZ + z}

    def pix_of(k):
        return lax.rem(x + k[0], NX) * NZ + lax.rem(z + k[1], NZ)

    def pix_peer(k):
        return {"gal": g, "pix": pix_of(k)}

    def chunk(k):
        return lax.rem(y + k, NY)

    def rows_of(k):
        return pl.ds(pl.multiple_of(chunk(k) * CHUNK, CHUNK), CHUNK)

    def loads(k):
        rows = rows_of(k)
        return [
            pltpu.make_async_copy(src.at[rows, :], dst.at[rows, :], load_sem.at[i, k])
            for i, (src, dst) in enumerate(((obs_hbm, obs), (sp_hbm, work), (du_hbm, dual)))
        ]

    load_right = pltpu.make_async_copy(right_hbm, right_ref, load_sem.at[3, 0])
    load_right.start()
    for k in ORDER:
        for copy in loads(k):
            copy.start()
    barrier = pltpu.get_barrier_semaphore()
    for k in PIX_ORDER:
        pl.semaphore_signal(barrier, inc=1, device_id=pix_peer(k), device_id_type=MESH)
    for k in range(1, NG):
        pl.semaphore_signal(barrier, inc=1, device_id=gal_peer(lax.rem(g + k, NG)), device_id_type=MESH)

    def send(it, kind, src, dst, peer, recv):
        pltpu.make_async_remote_copy(
            src_ref=src, dst_ref=dst, send_sem=send_sem.at[it, kind], recv_sem=recv,
            device_id=peer, device_id_type=MESH,
        ).start()

    def spread(it, kind, n, me, peer, src_of, dst):
        order = sorted(range(1, n), key=lambda k: -min(k, n - k))
        for k in order:
            t = lax.rem(me + k, n)
            send(it, kind, src_of(t), dst.at[it, me], peer(t), recv_sem.at[it, kind])

    def arrived(it, kind, n, dst):
        view = dst.at[it, pl.ds(0, n - 1)]
        pltpu.make_async_copy(view, view, recv_sem.at[it, kind]).wait()

    def landed(view, sem):
        pltpu.make_async_copy(view, view, sem).wait()

    def total(buf, it, n):
        acc = buf[it, 0]
        for i in range(1, n):
            acc = acc + buf[it, i]
        return acc

    def panel_chunk(it, k, r3, target):
        rows = rows_of(k)
        terms = split3(target)
        for dst, term in zip((thi, tmid, tlo), terms):
            dst[rows, :] = term
        p = mm3(r3, *terms, NT)
        first = 2 * chunk(k)
        part[it, first] = p[:, :GB]
        part[it, first + 1] = p[:, GB:]

    def to_partner(it, k):
        send(it, PEX, part.at[it, 2 * chunk(k) + other], pex.at[it, k], gal_peer(2 * y + other), pex_sem.at[it, k])

    def from_partner(it, k):
        landed(pex.at[it, k], pex_sem.at[it, k])
        d = 2 * chunk(k) + core
        part[it, d] = part[it, d] + pex[it, k]
        if k:
            send(it, PRS, part.at[it, d], prs.at[it, NY - k], gal_peer(d), recv_sem.at[it, PRS])

    with scope("load_right"):
        load_right.wait()
        r3 = stacked(right_ref[...])
    for k in ORDER:
        with scope("load"):
            for copy in loads(k):
                copy.wait()
        with scope("target"):
            rows = rows_of(k)
            c = dual[rows, :] * INV_MU
            dual[rows, :] = c
            target = obs[rows, :] - work[rows, :] + c
        with scope("panel"):
            panel_chunk(0, k, r3, target)
        if k == ORDER[0]:
            with scope("barrier"):
                pl.semaphore_wait(barrier, NG + NP - 2)
        to_partner(0, k)
        if k != ORDER[0]:
            from_partner(0, last)
        last = k
    from_partner(0, last)

    for it in range(2):
        if it == 1:
            with scope("w_gar"):
                arrived(0, GAR, NG, gall)
            with scope("chol_right"):
                inv_right = factor_of(total(gall, 0, NG))
        with scope("w_prs"):
            view = prs.at[it, pl.ds(1, NY - 1)]
            landed(view, recv_sem.at[it, PRS])
        with scope("pag_send"):
            mine = (part[it, g] + prs[it, 1]) + (prs[it, 2] + prs[it, 3])
            if it == 1:
                mine = product(inv_right, mine)
            panel[it, g] = mine
            own = panel.at[it, g]
            for k in (2, 1, 3):
                send(it, PAG, own, own, gal_peer(2 * chunk(k) + core), near_sem.at[it, NY - k])
            partner = gal_peer(2 * y + other)
            send(it, PAG, own, own, partner, near_sem.at[it, 0])
        with scope("gram_left"):
            gram = twin_gram(mine)
            for d in range(NG):
                kpart[it, d] = gram[d * RB : (d + 1) * RB]
            spread(it, KG, NG, g, gal_peer, lambda t: kpart.at[it, t], kg)
            kg[it, g] = kpart[it, g]

        def send_kz():
            with scope("w_kg"):
                arrived(it, KG, NG, kg)
            kz[it, z] = total(kg, it, NG)
            spread(it, KZ, NZ, z, z_peer, lambda t: kz.at[it, z], kz)

        raw = None

        def relay(k):
            with scope("w_relay"):
                slot = panel.at[it, 2 * chunk(k) + core]
                landed(slot, near_sem.at[it, k])
                send(it, PAG, slot, slot, partner, relay_sem.at[it, k])

        for k in (0, 1, 3, 2):
            block = 2 * chunk(k)
            rows = rows_of(k)
            with scope("w_near"):
                landed(panel.at[it, block + other], near_sem.at[it, 0] if k == 0 else relay_sem.at[it, k])
            with scope("norm"):
                p = jnp.concatenate([panel[it, block], panel[it, block + 1]], axis=1)
                normal[:, rows] = p
            with scope("raw_wide"):
                term = mm3(stacked(p), thi[rows, :], tmid[rows, :], tlo[rows, :], NN)
                raw = term if raw is None else raw + term
            if k == 0:
                relay(1)
                relay(3)
            elif k == 1:
                relay(2)
            if k == 1:
                send_kz()
        with scope("w_send"):
            for i in range(NX):
                for j in range(NZ):
                    wpart[it, i * NZ + j] = raw[j * RB : (j + 1) * RB, i * LB : (i + 1) * LB]
            for k in PIX_ORDER:
                send(it, WRS, wpart.at[it, pix_of(k)], wrs.at[it, pix], pix_peer(k), recv_sem.at[it, WRS])
            wrs[it, pix] = wpart[it, pix]

        with scope("w_kz"):
            arrived(it, KZ, NZ, kz)
        kx[it, x] = total(kz, it, NZ)
        spread(it, KX, NX, x, x_peer, lambda t: kx.at[it, x], kx)

        def finish_k():
            with scope("w_kx"):
                arrived(it, KX, NX, kx)
            kraw[it, g] = total(kx, it, NX)
            spread(it, KAG, NG, g, gal_peer, lambda t: kraw.at[it, g], kraw)

        with scope("w_wrs"):
            arrived(it, WRS, NP, wrs)
        with scope("wag_send"):
            wraw[it, pix] = total(wrs, it, NP)
            own = wraw.at[it, pix]
            for k in PIX_ORDER:
                send(it, WAG, own, own, pix_peer(k), recv_sem.at[it, WAG])
        finish_k()

        with scope("w_kag"):
            arrived(it, KAG, NG, kraw)
        with scope("chol_left"):
            inv_left = inverse_factor(jnp.concatenate([kraw[it, i] for i in range(NG)], axis=0))

        def put_left():
            with scope("left"):
                left = product(inv_left, normal[...])
                l_high, l_low = split(left)
                lstk[0:R, :] = l_high
                lstk[R : 2 * R, :] = l_high
                lstk[2 * R : 3 * R, :] = l_low
                if it == 1:
                    left_ref[...] = left

        if it == 0:
            put_left()
        with scope("w_wag"):
            arrived(it, WAG, NP, wraw)
        with scope("wide"):
            columns = [jnp.concatenate([wraw[it, i * NZ + j] for j in range(NZ)], axis=0) for i in range(NX)]
            wide = product(inv_left, jnp.concatenate(columns, axis=1))
            w_high, w_low = split(wide)
            wstk = jnp.concatenate([w_high, w_low, w_high], axis=0)
            r3 = stacked(wide)
        with scope("gram_right"):
            gram = twin_gram(wide)
            lane = lax.broadcasted_iota(jnp.int32, (R // 2, 128), 1)
            gall[it, g] = jnp.where(lane < R, gram[: R // 2], gram[R // 2 :])
            spread(it, GAR, NG, g, gal_peer, lambda t: gall.at[it, g], gall)
        if it == 1:
            put_left()
        for k in ORDER:
            with scope("update"):
                rows = rows_of(k)
                low = mm(lstk[:, rows], wstk, TN)
                c = dual[rows, :]
                if it == 0:
                    clipped = clip(obs[rows, :] + c - low)
                    dual[rows, :] = clipped
                    panel_chunk(1, k, r3, low - c + (clipped + clipped))
                    to_partner(1, k)
                    if k != ORDER[0]:
                        from_partner(1, last)
                    last = k
                else:
                    v = obs[rows, :] + c - low
                    clipped = clip(v)
                    sparse_out[rows, :] = v - clipped
                    dual_out[rows, :] = MU * clipped
        if it == 0:
            from_partner(1, last)

    wide_ref[...] = wide
    with scope("w_gar"):
        arrived(1, GAR, NG, gall)
    gram_ref[...] = total(gall, 1, NG)
    with scope("fin"):
        for it in range(2):
            for kind, n, buf in (
                (PEX, NY + 1, pex), (PRS, NY, prs), (PAG, NG, panel), (WRS, NP, wrs), (WAG, NP, wraw),
                (KG, NG, kg), (KZ, NZ, kz), (KX, NX, kx), (KAG, NG, kraw), (GAR, NG, gall),
            ):
                landed(buf.at[it, pl.ds(0, n - 1)], send_sem.at[it, kind])


def outputs(
    sparse, dual, left, wide, gram, sparse_hbm, dual_hbm, left_hbm, right_hbm, right, sem,
):
    copies = [
        pltpu.make_async_copy(src, dst, sem.at[i])
        for i, (src, dst) in enumerate(((sparse, sparse_hbm), (dual, dual_hbm), (left, left_hbm), (right, right_hbm)))
    ]
    for copy in copies[:3]:
        copy.start()
    right[...] = product(factor_of(gram[...]), wide[...])
    copies[3].start()
    for copy in copies:
        copy.wait()


def per_device(observed, sparse_init, dual_init, right_init):
    hbm = pl.BlockSpec(memory_space=pltpu.HBM)
    vmem = pl.BlockSpec(memory_space=pltpu.VMEM)
    shape = (ROWS, COLS)
    whole = jax.ShapeDtypeStruct(shape, F32)
    left_shape = jax.ShapeDtypeStruct((R, ROWS), F32)
    right_shape = jax.ShapeDtypeStruct((R, COLS), F32)
    state = pl.pallas_call(
        kernel,
        out_shape=(whole, whole, left_shape, right_shape, jax.ShapeDtypeStruct((R // 2, 2 * R), F32)),
        in_specs=[hbm] * 4,
        out_specs=(vmem,) * 5,
        scratch_shapes=[
            pltpu.VMEM((R, COLS), F32),
            pltpu.VMEM(shape, F32),
            pltpu.VMEM(shape, F32),
            pltpu.VMEM(shape, F32),
            pltpu.VMEM(shape, BF16),
            pltpu.VMEM(shape, BF16),
            pltpu.VMEM(shape, BF16),
            pltpu.VMEM((3 * R, ROWS), BF16),
            pltpu.VMEM((2, NG, R, GB), F32),
            pltpu.VMEM((2, NY, R, GB), F32),
            pltpu.VMEM((2, NY, R, GB), F32),
            pltpu.VMEM((2, NG, R, GB), F32),
            pltpu.VMEM((R, ROWS), F32),
            pltpu.VMEM((2, NP, RB, LB), F32),
            pltpu.VMEM((2, NP, RB, LB), F32),
            pltpu.VMEM((2, NP, RB, LB), F32),
            pltpu.VMEM((2, NG, RB, 2 * R), F32),
            pltpu.VMEM((2, NG, RB, 2 * R), F32),
            pltpu.VMEM((2, NZ, RB, 2 * R), F32),
            pltpu.VMEM((2, NX, RB, 2 * R), F32),
            pltpu.VMEM((2, NG, RB, 2 * R), F32),
            pltpu.VMEM((2, NG, R // 2, 2 * R), F32),
            pltpu.SemaphoreType.DMA((4, NY)),
            pltpu.SemaphoreType.DMA((2, 10)),
            pltpu.SemaphoreType.DMA((2, 10)),
            pltpu.SemaphoreType.DMA((2, NY)),
            pltpu.SemaphoreType.DMA((2, NY)),
            pltpu.SemaphoreType.DMA((2, NY)),
        ],
        compiler_params=pltpu.CompilerParams(collective_id=0, has_side_effects=True, vmem_limit_bytes=48 << 20),
        name="pursuit",
    )(*(pltpu.with_memory_space_constraint(a, pltpu.HBM) for a in (observed, sparse_init, dual_init, right_init)))
    return pl.pallas_call(
        outputs,
        out_shape=(whole, whole, left_shape, right_shape),
        in_specs=[vmem] * 5,
        out_specs=(hbm,) * 4,
        scratch_shapes=[
            pltpu.VMEM((R, COLS), F32),
            pltpu.SemaphoreType.DMA((4,)),
        ],
        compiler_params=pltpu.CompilerParams(vmem_limit_bytes=24 << 20),
        name="outputs",
    )(*state)


def solution(mesh):
    return jax.shard_map(
        per_device,
        mesh=mesh,
        in_specs=(P("pix", "gal"), P("pix", "gal"), P("pix", "gal"), P(None, "gal")),
        out_specs=(P("pix", "gal"), P("pix", "gal"), P(None, "pix"), P(None, "gal")),
        check_vma=False,
    )
```

```python
import contextlib

import jax
import jax.numpy as jnp
from jax import lax
from jax.experimental import pallas as pl
from jax.experimental.pallas import tpu as pltpu
from jax.sharding import PartitionSpec as P

MU = 1.25
TAU = 0.6 / 1.25
INV_MU = 1.0 / MU
HIGH = lax.Precision.HIGHEST
MESH = pl.DeviceIdType.MESH
F32 = jnp.float32
BF16 = jnp.bfloat16

NY = 4
NG = 8
NZ = 8
NX = 4
NP = NZ * NX
R = 64
ROWS = 1024
COLS = 512
GB = ROWS // NG
RB = 8
LB = 128
CHUNK = ROWS // NY
ORDER = (2, 1, 3, 0)

PIX_ORDER = sorted(
    ((i, j) for i in range(NX) for j in range(NZ) if i or j), key=lambda k: -(min(k[0], NX - k[0]) + min(k[1], NZ - k[1]))
)

PEX, PRS, PAG, WRS, WAG, KG, KZ, KX, KAG, GAR = range(10)

NN = (((1,), (0,)), ((), ()))
NT = (((1,), (1,)), ((), ()))
TN = (((0,), (0,)), ((), ()))


def split(value):
    high = value.astype(BF16)
    return high, (value - high.astype(F32)).astype(BF16)


def split3(value):
    high = value.astype(BF16)
    mid, low = split(value - high.astype(F32))
    return high, mid, low


def mm(a, b, dims):
    return lax.dot_general(a, b, dims, preferred_element_type=F32)


def mm_high(a, b, dims):
    return lax.dot_general(a, b, dims, precision=HIGH, preferred_element_type=F32)


def twin_gram(value):
    high, mid, low = split3(value)
    out = mm(jnp.concatenate([high, mid, low], axis=0), jnp.concatenate([high, high, mid, mid, low, low], axis=0), NT)
    out = out[:R] + (out[R : 2 * R] + out[2 * R :])
    return out[:, : 2 * R] + (out[:, 2 * R : 4 * R] + out[:, 4 * R :])


def stacked(value):
    return jnp.concatenate(split3(value), axis=0)


def mm3(a, high, mid, low, dims):
    first = mm(a, high, dims)
    second = mm(a[: 2 * R], mid, dims)
    third = mm(a[:R], low, dims)
    return first[:R] + ((first[R : 2 * R] + second[:R]) + (first[2 * R :] + second[R:] + third))


def clip(value):
    return jnp.minimum(jnp.maximum(value, -TAU), TAU)


def solver(e00, e01, e02, e03, e11, e12, e13, e22, e23, e33):
    det = e00 * e11 - e01 * e01
    inv = 1.0 / det
    n00, n01, n11 = e11 * inv, -(e01 * inv), e00 * inv
    x00, x01 = n00 * e02 + n01 * e12, n00 * e03 + n01 * e13
    x10, x11 = n01 * e02 + n11 * e12, n01 * e03 + n11 * e13
    s00 = e22 - (e02 * x00 + e12 * x10)
    s01 = e23 - (e02 * x01 + e12 * x11)
    s11 = e33 - (e03 * x01 + e13 * x11)
    sdet = s00 * s11 - s01 * s01
    sinv = 1.0 / sdet
    m00, m01, m11 = s11 * sinv, -(s01 * sinv), s00 * sinv

    def reduce(v0, v1, v2, v3):
        return v2 - (x00 * v0 + x10 * v1), v3 - (x01 * v0 + x11 * v1)

    def solve(v0, v1, v2, v3):
        u2, u3 = reduce(v0, v1, v2, v3)
        y2, y3 = m00 * u2 + m01 * u3, m01 * u2 + m11 * u3
        y0 = (n00 * v0 + n01 * v1) - (x00 * y2 + x01 * y3)
        y1 = (n01 * v0 + n11 * v1) - (x10 * y2 + x11 * y3)
        return y0, y1, y2, y3

    def factor(v0, v1, v2, v3):
        u2, u3 = reduce(v0, v1, v2, v3)
        return (
            v0 * (1.0 / jnp.sqrt(e00)),
            (v1 - (e01 / e00) * v0) * (1.0 / jnp.sqrt(det / e00)),
            u2 * (1.0 / jnp.sqrt(s00)),
            (u3 - (s01 / s00) * u2) * (1.0 / jnp.sqrt(sdet / s00)),
        )

    return solve, factor


def inverse_factor(gram2):
    tile = (8, 128)
    lane = lax.broadcasted_iota(jnp.int32, tile, 1)
    sub = lax.broadcasted_iota(jnp.int32, tile, 0)
    zero = jnp.minimum(jnp.abs(gram2[:8, :]), 0.0)
    tiles, out = [], []
    for b in range(8):
        eye = jnp.where(lane == sub + 8 * b, 1.0, 0.0)
        tiles.append(jnp.where(lane < R, eye, gram2[8 * b : 8 * b + 8, :]))

    def row(value, p):
        return jnp.broadcast_to(value[p : p + 1, :], tile)

    def four(e, first):
        return [e[first + p, first + q] for p in range(4) for q in range(p, 4)]

    for t in range(8):
        columns = [
            [jnp.broadcast_to(tiles[b][:, R + 8 * t + q : R + 8 * t + q + 1], tile) for q in range(8)] for b in range(t, 8)
        ]
        rows = [row(tiles[t], p) for p in range(8)]
        e = {}
        for q in range(8):
            spread_column = columns[0][q] + zero
            for p in range(q + 1):
                e[p, q] = row(spread_column, p)
        solve, factor = solver(*four(e, 0))
        upper = rows[:4]
        y = solve(*upper)
        cross = [solve(*(e[r, q] for r in range(4))) for q in range(4, 8)]

        def less(value, p, ys):
            return value - ((e[0, p] * ys[0] + e[1, p] * ys[1]) + (e[2, p] * ys[2] + e[3, p] * ys[3]))

        late = {(p, q): less(e[p, q], p, cross[q - 4]) for q in range(4, 8) for p in range(4, q + 1)}
        lower = [less(rows[p], p, y) for p in range(4, 8)]
        solve_late, factor_late = solver(*four(late, 4))
        done = [*factor(*upper), *factor_late(*lower)]
        result = done[7]
        for p in range(6, -1, -1):
            result = jnp.where(sub == p, done[p], result)
        out.append(result)
        if t < 7:
            w = solve_late(*lower)
            full = [
                y[r] - ((cross[0][r] * w[0] + cross[1][r] * w[1]) + (cross[2][r] * w[2] + cross[3][r] * w[3]))
                for r in range(4)
            ] + list(w)
            for b in range(t + 1, 8):
                terms = [columns[b - t][q] * full[q] for q in range(8)]
                tiles[b] = tiles[b] - (
                    ((terms[0] + terms[1]) + (terms[2] + terms[3])) + ((terms[4] + terms[5]) + (terms[6] + terms[7]))
                )
    return jnp.concatenate(out, axis=0)


def product(inverse, value):
    return mm_high(inverse[:, :R], value, NN)


def factor_of(packed):
    return inverse_factor(jnp.concatenate([pltpu.roll(packed, R, 1), packed], axis=0))


def scope(name):
    return contextlib.nullcontext()


def kernel(
    obs_hbm, sp_hbm, du_hbm, right_hbm, sparse_out, dual_out, left_ref, wide_ref, gram_ref,
    right_ref, obs, work, dual, thi, tmid, tlo, lstk,
    part, pex, prs, panel, normal, wpart, wrs, wraw, kpart, kg, kz, kx, kraw, gall,
    load_sem, send_sem, recv_sem, pex_sem, near_sem, relay_sem,
):
    g = lax.axis_index("gal")
    pix = lax.axis_index("pix")
    y, core = lax.div(g, 2), lax.rem(g, 2)
    other = 1 - core
    z = lax.rem(pix, NZ)
    x = lax.div(pix, NZ)

    def gal_peer(t):
        return {"gal": t, "pix": pix}

    def z_peer(t):
        return {"gal": g, "pix": x * NZ + t}

    def x_peer(t):
        return {"gal": g, "pix": t * NZ + z}

    def pix_of(k):
        return lax.rem(x + k[0], NX) * NZ + lax.rem(z + k[1], NZ)

    def pix_peer(k):
        return {"gal": g, "pix": pix_of(k)}

    def chunk(k):
        return lax.rem(y + k, NY)

    def rows_of(k):
        return pl.ds(pl.multiple_of(chunk(k) * CHUNK, CHUNK), CHUNK)

    def loads(k):
        rows = rows_of(k)
        return [
            pltpu.make_async_copy(src.at[rows, :], dst.at[rows, :], load_sem.at[i, k])
            for i, (src, dst) in enumerate(((obs_hbm, obs), (sp_hbm, work), (du_hbm, dual)))
        ]

    load_right = pltpu.make_async_copy(right_hbm, right_ref, load_sem.at[3, 0])
    load_right.start()
    for k in ORDER:
        for copy in loads(k):
            copy.start()
    barrier = pltpu.get_barrier_semaphore()
    for k in PIX_ORDER:
        pl.semaphore_signal(barrier, inc=1, device_id=pix_peer(k), device_id_type=MESH)
    for k in range(1, NG):
        pl.semaphore_signal(barrier, inc=1, device_id=gal_peer(lax.rem(g + k, NG)), device_id_type=MESH)

    def send(it, kind, src, dst, peer, recv):
        pltpu.make_async_remote_copy(
            src_ref=src, dst_ref=dst, send_sem=send_sem.at[it, kind], recv_sem=recv,
            device_id=peer, device_id_type=MESH,
        ).start()

    def spread(it, kind, n, me, peer, src_of, dst):
        order = sorted(range(1, n), key=lambda k: -min(k, n - k))
        for k in order:
            t = lax.rem(me + k, n)
            send(it, kind, src_of(t), dst.at[it, me], peer(t), recv_sem.at[it, kind])

    def arrived(it, kind, n, dst):
        view = dst.at[it, pl.ds(0, n - 1)]
        pltpu.make_async_copy(view, view, recv_sem.at[it, kind]).wait()

    def landed(view, sem):
        pltpu.make_async_copy(view, view, sem).wait()

    def total(buf, it, n):
        acc = buf[it, 0]
        for i in range(1, n):
            acc = acc + buf[it, i]
        return acc

    def panel_chunk(it, k, r3, target):
        rows = rows_of(k)
        terms = split3(target)
        for dst, term in zip((thi, tmid, tlo), terms):
            dst[rows, :] = term
        p = mm3(r3, *terms, NT)
        first = 2 * chunk(k)
        part[it, first] = p[:, :GB]
        part[it, first + 1] = p[:, GB:]

    def to_partner(it, k):
        send(it, PEX, part.at[it, 2 * chunk(k) + other], pex.at[it, k], gal_peer(2 * y + other), pex_sem.at[it, k])

    def from_partner(it, k):
        landed(pex.at[it, k], pex_sem.at[it, k])
        d = 2 * chunk(k) + core
        part[it, d] = part[it, d] + pex[it, k]
        if k:
            send(it, PRS, part.at[it, d], prs.at[it, NY - k], gal_peer(d), recv_sem.at[it, PRS])

    with scope("load_right"):
        load_right.wait()
        r3 = stacked(right_ref[...])
    for k in ORDER:
        with scope("load"):
            for copy in loads(k):
                copy.wait()
        with scope("target"):
            rows = rows_of(k)
            c = dual[rows, :] * INV_MU
            dual[rows, :] = c
            target = obs[rows, :] - work[rows, :] + c
        with scope("panel"):
            panel_chunk(0, k, r3, target)
        if k == ORDER[0]:
            with scope("barrier"):
                pl.semaphore_wait(barrier, NG + NP - 2)
        to_partner(0, k)
        if k != ORDER[0]:
            from_partner(0, last)
        last = k
    from_partner(0, last)

    for it in range(2):
        if it == 1:
            with scope("w_gar"):
                arrived(0, GAR, NG, gall)
            with scope("chol_right"):
                inv_right = factor_of(total(gall, 0, NG))
        with scope("w_prs"):
            view = prs.at[it, pl.ds(1, NY - 1)]
            landed(view, recv_sem.at[it, PRS])
        with scope("pag_send"):
            mine = (part[it, g] + prs[it, 1]) + (prs[it, 2] + prs[it, 3])
            if it == 1:
                mine = product(inv_right, mine)
            panel[it, g] = mine
            own = panel.at[it, g]
            for k in (2, 1, 3):
                send(it, PAG, own, own, gal_peer(2 * chunk(k) + core), near_sem.at[it, NY - k])
            partner = gal_peer(2 * y + other)
            send(it, PAG, own, own, partner, near_sem.at[it, 0])
        with scope("gram_left"):
            gram = twin_gram(mine)
            for d in range(NG):
                kpart[it, d] = gram[d * RB : (d + 1) * RB]
            spread(it, KG, NG, g, gal_peer, lambda t: kpart.at[it, t], kg)
            kg[it, g] = kpart[it, g]

        def send_kz():
            with scope("w_kg"):
                arrived(it, KG, NG, kg)
            kz[it, z] = total(kg, it, NG)
            spread(it, KZ, NZ, z, z_peer, lambda t: kz.at[it, z], kz)

        raw = None

        def relay(k):
            with scope("w_relay"):
                slot = panel.at[it, 2 * chunk(k) + core]
                landed(slot, near_sem.at[it, k])
                send(it, PAG, slot, slot, partner, relay_sem.at[it, k])

        for k in (0, 1, 3, 2):
            block = 2 * chunk(k)
            rows = rows_of(k)
            with scope("w_near"):
                landed(panel.at[it, block + other], near_sem.at[it, 0] if k == 0 else relay_sem.at[it, k])
            with scope("norm"):
                p = jnp.concatenate([panel[it, block], panel[it, block + 1]], axis=1)
                normal[:, rows] = p
            with scope("raw_wide"):
                term = mm3(stacked(p), thi[rows, :], tmid[rows, :], tlo[rows, :], NN)
                raw = term if raw is None else raw + term
            if k == 0:
                for kk in (1, 3, 2):
                    relay(kk)
            if k == 3:
                send_kz()
        with scope("w_send"):
            for i in range(NX):
                for j in range(NZ):
                    wpart[it, i * NZ + j] = raw[j * RB : (j + 1) * RB, i * LB : (i + 1) * LB]
            for k in PIX_ORDER:
                send(it, WRS, wpart.at[it, pix_of(k)], wrs.at[it, pix], pix_peer(k), recv_sem.at[it, WRS])
            wrs[it, pix] = wpart[it, pix]

        with scope("w_kz"):
            arrived(it, KZ, NZ, kz)
        kx[it, x] = total(kz, it, NZ)
        spread(it, KX, NX, x, x_peer, lambda t: kx.at[it, x], kx)

        def finish_k():
            with scope("w_kx"):
                arrived(it, KX, NX, kx)
            kraw[it, g] = total(kx, it, NX)
            spread(it, KAG, NG, g, gal_peer, lambda t: kraw.at[it, g], kraw)

        with scope("w_wrs"):
            arrived(it, WRS, NP, wrs)
        with scope("wag_send"):
            wraw[it, pix] = total(wrs, it, NP)
            own = wraw.at[it, pix]
            for k in PIX_ORDER:
                send(it, WAG, own, own, pix_peer(k), recv_sem.at[it, WAG])
        finish_k()

        with scope("w_kag"):
            arrived(it, KAG, NG, kraw)
        with scope("chol_left"):
            inv_left = inverse_factor(jnp.concatenate([kraw[it, i] for i in range(NG)], axis=0))

        def put_left():
            with scope("left"):
                left = product(inv_left, normal[...])
                l_high, l_low = split(left)
                lstk[0:R, :] = l_high
                lstk[R : 2 * R, :] = l_high
                lstk[2 * R : 3 * R, :] = l_low
                if it == 1:
                    left_ref[...] = left

        if it == 0:
            put_left()
        with scope("w_wag"):
            arrived(it, WAG, NP, wraw)
        with scope("wide"):
            columns = [jnp.concatenate([wraw[it, i * NZ + j] for j in range(NZ)], axis=0) for i in range(NX)]
            wide = product(inv_left, jnp.concatenate(columns, axis=1))
            w_high, w_low = split(wide)
            wstk = jnp.concatenate([w_high, w_low, w_high], axis=0)
            r3 = stacked(wide)
        with scope("gram_right"):
            gram = twin_gram(wide)
            lane = lax.broadcasted_iota(jnp.int32, (R // 2, 128), 1)
            gall[it, g] = jnp.where(lane < R, gram[: R // 2], gram[R // 2 :])
            spread(it, GAR, NG, g, gal_peer, lambda t: gall.at[it, g], gall)
        if it == 1:
            put_left()
        for k in ORDER:
            with scope("update"):
                rows = rows_of(k)
                low = mm(lstk[:, rows], wstk, TN)
                c = dual[rows, :]
                if it == 0:
                    clipped = clip(obs[rows, :] + c - low)
                    dual[rows, :] = clipped
                    panel_chunk(1, k, r3, low - c + (clipped + clipped))
                    to_partner(1, k)
                    if k != ORDER[0]:
                        from_partner(1, last)
                    last = k
                else:
                    v = obs[rows, :] + c - low
                    clipped = clip(v)
                    sparse_out[rows, :] = v - clipped
                    dual_out[rows, :] = MU * clipped
        if it == 0:
            from_partner(1, last)

    wide_ref[...] = wide
    with scope("w_gar"):
        arrived(1, GAR, NG, gall)
    gram_ref[...] = total(gall, 1, NG)
    with scope("fin"):
        for it in range(2):
            for kind, n, buf in (
                (PEX, NY + 1, pex), (PRS, NY, prs), (PAG, NG, panel), (WRS, NP, wrs), (WAG, NP, wraw),
                (KG, NG, kg), (KZ, NZ, kz), (KX, NX, kx), (KAG, NG, kraw), (GAR, NG, gall),
            ):
                landed(buf.at[it, pl.ds(0, n - 1)], send_sem.at[it, kind])


def outputs(
    sparse, dual, left, wide, gram, sparse_hbm, dual_hbm, left_hbm, right_hbm, right, sem,
):
    copies = [
        pltpu.make_async_copy(src, dst, sem.at[i])
        for i, (src, dst) in enumerate(((sparse, sparse_hbm), (dual, dual_hbm), (left, left_hbm), (right, right_hbm)))
    ]
    for copy in copies[:3]:
        copy.start()
    right[...] = product(factor_of(gram[...]), wide[...])
    copies[3].start()
    for copy in copies:
        copy.wait()


def per_device(observed, sparse_init, dual_init, right_init):
    hbm = pl.BlockSpec(memory_space=pltpu.HBM)
    vmem = pl.BlockSpec(memory_space=pltpu.VMEM)
    shape = (ROWS, COLS)
    whole = jax.ShapeDtypeStruct(shape, F32)
    left_shape = jax.ShapeDtypeStruct((R, ROWS), F32)
    right_shape = jax.ShapeDtypeStruct((R, COLS), F32)
    state = pl.pallas_call(
        kernel,
        out_shape=(whole, whole, left_shape, right_shape, jax.ShapeDtypeStruct((R // 2, 2 * R), F32)),
        in_specs=[hbm] * 4,
        out_specs=(vmem,) * 5,
        scratch_shapes=[
            pltpu.VMEM((R, COLS), F32),
            pltpu.VMEM(shape, F32),
            pltpu.VMEM(shape, F32),
            pltpu.VMEM(shape, F32),
            pltpu.VMEM(shape, BF16),
            pltpu.VMEM(shape, BF16),
            pltpu.VMEM(shape, BF16),
            pltpu.VMEM((3 * R, ROWS), BF16),
            pltpu.VMEM((2, NG, R, GB), F32),
            pltpu.VMEM((2, NY, R, GB), F32),
            pltpu.VMEM((2, NY, R, GB), F32),
            pltpu.VMEM((2, NG, R, GB), F32),
            pltpu.VMEM((R, ROWS), F32),
            pltpu.VMEM((2, NP, RB, LB), F32),
            pltpu.VMEM((2, NP, RB, LB), F32),
            pltpu.VMEM((2, NP, RB, LB), F32),
            pltpu.VMEM((2, NG, RB, 2 * R), F32),
            pltpu.VMEM((2, NG, RB, 2 * R), F32),
            pltpu.VMEM((2, NZ, RB, 2 * R), F32),
            pltpu.VMEM((2, NX, RB, 2 * R), F32),
            pltpu.VMEM((2, NG, RB, 2 * R), F32),
            pltpu.VMEM((2, NG, R // 2, 2 * R), F32),
            pltpu.SemaphoreType.DMA((4, NY)),
            pltpu.SemaphoreType.DMA((2, 10)),
            pltpu.SemaphoreType.DMA((2, 10)),
            pltpu.SemaphoreType.DMA((2, NY)),
            pltpu.SemaphoreType.DMA((2, NY)),
            pltpu.SemaphoreType.DMA((2, NY)),
        ],
        compiler_params=pltpu.CompilerParams(collective_id=0, has_side_effects=True, vmem_limit_bytes=48 << 20),
        name="pursuit",
    )(*(pltpu.with_memory_space_constraint(a, pltpu.HBM) for a in (observed, sparse_init, dual_init, right_init)))
    return pl.pallas_call(
        outputs,
        out_shape=(whole, whole, left_shape, right_shape),
        in_specs=[vmem] * 5,
        out_specs=(hbm,) * 4,
        scratch_shapes=[
            pltpu.VMEM((R, COLS), F32),
            pltpu.SemaphoreType.DMA((4,)),
        ],
        compiler_params=pltpu.CompilerParams(vmem_limit_bytes=24 << 20),
        name="outputs",
    )(*state)


def solution(mesh):
    return jax.shard_map(
        per_device,
        mesh=mesh,
        in_specs=(P("pix", "gal"), P("pix", "gal"), P("pix", "gal"), P(None, "gal")),
        out_specs=(P("pix", "gal"), P("pix", "gal"), P(None, "pix"), P(None, "gal")),
        check_vma=False,
    )
```

```python
import contextlib

import jax
import jax.numpy as jnp
from jax import lax
from jax.experimental import pallas as pl
from jax.experimental.pallas import tpu as pltpu
from jax.sharding import PartitionSpec as P

MU = 1.25
TAU = 0.6 / 1.25
INV_MU = 1.0 / MU
HIGH = lax.Precision.HIGHEST
MESH = pl.DeviceIdType.MESH
F32 = jnp.float32
BF16 = jnp.bfloat16

NY = 4
NG = 8
NZ = 8
NX = 4
NP = NZ * NX
R = 64
ROWS = 1024
COLS = 512
GB = ROWS // NG
RB = 8
LB = 128
CHUNK = ROWS // NY
ORDER = (2, 1, 3, 0)

PIX_ORDER = sorted(
    ((i, j) for i in range(NX) for j in range(NZ) if i or j), key=lambda k: -(min(k[0], NX - k[0]) + min(k[1], NZ - k[1]))
)

PEX, PRS, PAG, WRS, WAG, KG, KZ, KX, KAG, GAR = range(10)

NN = (((1,), (0,)), ((), ()))
NT = (((1,), (1,)), ((), ()))
TN = (((0,), (0,)), ((), ()))


def split(value):
    high = value.astype(BF16)
    return high, (value - high.astype(F32)).astype(BF16)


def split3(value):
    high = value.astype(BF16)
    mid, low = split(value - high.astype(F32))
    return high, mid, low


def mm(a, b, dims):
    return lax.dot_general(a, b, dims, preferred_element_type=F32)


def mm_high(a, b, dims):
    return lax.dot_general(a, b, dims, precision=HIGH, preferred_element_type=F32)


def twin_gram(value):
    high, mid, low = split3(value)
    out = mm(jnp.concatenate([high, mid, low], axis=0), jnp.concatenate([high, high, mid, mid, low, low], axis=0), NT)
    out = out[:R] + (out[R : 2 * R] + out[2 * R :])
    return out[:, : 2 * R] + (out[:, 2 * R : 4 * R] + out[:, 4 * R :])


def stacked(value):
    return jnp.concatenate(split3(value), axis=0)


def mm3(a, high, mid, low, dims):
    first = mm(a, high, dims)
    second = mm(a[: 2 * R], mid, dims)
    third = mm(a[:R], low, dims)
    return first[:R] + ((first[R : 2 * R] + second[:R]) + (first[2 * R :] + second[R:] + third))


def clip(value):
    return jnp.minimum(jnp.maximum(value, -TAU), TAU)


def solver(e00, e01, e02, e03, e11, e12, e13, e22, e23, e33):
    det = e00 * e11 - e01 * e01
    inv = 1.0 / det
    n00, n01, n11 = e11 * inv, -(e01 * inv), e00 * inv
    x00, x01 = n00 * e02 + n01 * e12, n00 * e03 + n01 * e13
    x10, x11 = n01 * e02 + n11 * e12, n01 * e03 + n11 * e13
    s00 = e22 - (e02 * x00 + e12 * x10)
    s01 = e23 - (e02 * x01 + e12 * x11)
    s11 = e33 - (e03 * x01 + e13 * x11)
    sdet = s00 * s11 - s01 * s01
    sinv = 1.0 / sdet
    m00, m01, m11 = s11 * sinv, -(s01 * sinv), s00 * sinv

    def reduce(v0, v1, v2, v3):
        return v2 - (x00 * v0 + x10 * v1), v3 - (x01 * v0 + x11 * v1)

    def solve(v0, v1, v2, v3):
        u2, u3 = reduce(v0, v1, v2, v3)
        y2, y3 = m00 * u2 + m01 * u3, m01 * u2 + m11 * u3
        y0 = (n00 * v0 + n01 * v1) - (x00 * y2 + x01 * y3)
        y1 = (n01 * v0 + n11 * v1) - (x10 * y2 + x11 * y3)
        return y0, y1, y2, y3

    def factor(v0, v1, v2, v3):
        u2, u3 = reduce(v0, v1, v2, v3)
        return (
            v0 * (1.0 / jnp.sqrt(e00)),
            (v1 - (e01 / e00) * v0) * (1.0 / jnp.sqrt(det / e00)),
            u2 * (1.0 / jnp.sqrt(s00)),
            (u3 - (s01 / s00) * u2) * (1.0 / jnp.sqrt(sdet / s00)),
        )

    return solve, factor


def inverse_factor(gram2):
    tile = (8, 128)
    lane = lax.broadcasted_iota(jnp.int32, tile, 1)
    sub = lax.broadcasted_iota(jnp.int32, tile, 0)
    zero = jnp.minimum(jnp.abs(gram2[:8, :]), 0.0)
    tiles, out = [], []
    for b in range(8):
        eye = jnp.where(lane == sub + 8 * b, 1.0, 0.0)
        tiles.append(jnp.where(lane < R, eye, gram2[8 * b : 8 * b + 8, :]))

    def row(value, p):
        return jnp.broadcast_to(value[p : p + 1, :], tile)

    def four(e, first):
        return [e[first + p, first + q] for p in range(4) for q in range(p, 4)]

    for t in range(8):
        columns = [
            [jnp.broadcast_to(tiles[b][:, R + 8 * t + q : R + 8 * t + q + 1], tile) for q in range(8)] for b in range(t, 8)
        ]
        rows = [row(tiles[t], p) for p in range(8)]
        e = {}
        for q in range(8):
            spread_column = columns[0][q] + zero
            for p in range(q + 1):
                e[p, q] = row(spread_column, p)
        solve, factor = solver(*four(e, 0))
        upper = rows[:4]
        y = solve(*upper)
        cross = [solve(*(e[r, q] for r in range(4))) for q in range(4, 8)]

        def less(value, p, ys):
            return value - ((e[0, p] * ys[0] + e[1, p] * ys[1]) + (e[2, p] * ys[2] + e[3, p] * ys[3]))

        late = {(p, q): less(e[p, q], p, cross[q - 4]) for q in range(4, 8) for p in range(4, q + 1)}
        lower = [less(rows[p], p, y) for p in range(4, 8)]
        solve_late, factor_late = solver(*four(late, 4))
        done = [*factor(*upper), *factor_late(*lower)]
        result = done[7]
        for p in range(6, -1, -1):
            result = jnp.where(sub == p, done[p], result)
        out.append(result)
        if t < 7:
            w = solve_late(*lower)
            full = [
                y[r] - ((cross[0][r] * w[0] + cross[1][r] * w[1]) + (cross[2][r] * w[2] + cross[3][r] * w[3]))
                for r in range(4)
            ] + list(w)
            for b in range(t + 1, 8):
                terms = [columns[b - t][q] * full[q] for q in range(8)]
                tiles[b] = tiles[b] - (
                    ((terms[0] + terms[1]) + (terms[2] + terms[3])) + ((terms[4] + terms[5]) + (terms[6] + terms[7]))
                )
    return jnp.concatenate(out, axis=0)


def product(inverse, value):
    return mm_high(inverse[:, :R], value, NN)


def factor_of(packed):
    return inverse_factor(jnp.concatenate([pltpu.roll(packed, R, 1), packed], axis=0))


def scope(name):
    return contextlib.nullcontext()


def kernel(
    obs_hbm, sp_hbm, du_hbm, right_hbm, sparse_out, dual_out, left_ref, wide_ref, gram_ref,
    right_ref, obs, work, dual, thi, tmid, tlo, lstk,
    part, pex, prs, panel, normal, wpart, wrs, wraw, kpart, kg, kz, kx, kraw, gall,
    load_sem, send_sem, recv_sem, pex_sem, near_sem, relay_sem,
):
    g = lax.axis_index("gal")
    pix = lax.axis_index("pix")
    y, core = lax.div(g, 2), lax.rem(g, 2)
    other = 1 - core
    z = lax.rem(pix, NZ)
    x = lax.div(pix, NZ)

    def gal_peer(t):
        return {"gal": t, "pix": pix}

    def z_peer(t):
        return {"gal": g, "pix": x * NZ + t}

    def x_peer(t):
        return {"gal": g, "pix": t * NZ + z}

    def pix_of(k):
        return lax.rem(x + k[0], NX) * NZ + lax.rem(z + k[1], NZ)

    def pix_peer(k):
        return {"gal": g, "pix": pix_of(k)}

    def chunk(k):
        return lax.rem(y + k, NY)

    def rows_of(k):
        return pl.ds(pl.multiple_of(chunk(k) * CHUNK, CHUNK), CHUNK)

    def loads(k):
        rows = rows_of(k)
        return [
            pltpu.make_async_copy(src.at[rows, :], dst.at[rows, :], load_sem.at[i, k])
            for i, (src, dst) in enumerate(((obs_hbm, obs), (sp_hbm, work), (du_hbm, dual)))
        ]

    load_right = pltpu.make_async_copy(right_hbm, right_ref, load_sem.at[3, 0])
    load_right.start()
    for k in ORDER:
        for copy in loads(k):
            copy.start()
    barrier = pltpu.get_barrier_semaphore()
    for k in PIX_ORDER:
        pl.semaphore_signal(barrier, inc=1, device_id=pix_peer(k), device_id_type=MESH)
    for k in range(1, NG):
        pl.semaphore_signal(barrier, inc=1, device_id=gal_peer(lax.rem(g + k, NG)), device_id_type=MESH)

    def send(it, kind, src, dst, peer, recv):
        pltpu.make_async_remote_copy(
            src_ref=src, dst_ref=dst, send_sem=send_sem.at[it, kind], recv_sem=recv,
            device_id=peer, device_id_type=MESH,
        ).start()

    def spread(it, kind, n, me, peer, src_of, dst):
        order = sorted(range(1, n), key=lambda k: -min(k, n - k))
        for k in order:
            t = lax.rem(me + k, n)
            send(it, kind, src_of(t), dst.at[it, me], peer(t), recv_sem.at[it, kind])

    def arrived(it, kind, n, dst):
        view = dst.at[it, pl.ds(0, n - 1)]
        pltpu.make_async_copy(view, view, recv_sem.at[it, kind]).wait()

    def landed(view, sem):
        pltpu.make_async_copy(view, view, sem).wait()

    def total(buf, it, n):
        acc = buf[it, 0]
        for i in range(1, n):
            acc = acc + buf[it, i]
        return acc

    def panel_chunk(it, k, r3, target):
        rows = rows_of(k)
        terms = split3(target)
        for dst, term in zip((thi, tmid, tlo), terms):
            dst[rows, :] = term
        p = mm3(r3, *terms, NT)
        first = 2 * chunk(k)
        part[it, first] = p[:, :GB]
        part[it, first + 1] = p[:, GB:]

    def to_partner(it, k):
        send(it, PEX, part.at[it, 2 * chunk(k) + other], pex.at[it, k], gal_peer(2 * y + other), pex_sem.at[it, k])

    def from_partner(it, k):
        landed(pex.at[it, k], pex_sem.at[it, k])
        d = 2 * chunk(k) + core
        part[it, d] = part[it, d] + pex[it, k]
        if k:
            send(it, PRS, part.at[it, d], prs.at[it, NY - k], gal_peer(d), recv_sem.at[it, PRS])

    with scope("load_right"):
        load_right.wait()
        r3 = stacked(right_ref[...])
    for k in ORDER:
        with scope("load"):
            for copy in loads(k):
                copy.wait()
        with scope("target"):
            rows = rows_of(k)
            c = dual[rows, :] * INV_MU
            dual[rows, :] = c
            target = obs[rows, :] - work[rows, :] + c
        with scope("panel"):
            panel_chunk(0, k, r3, target)
        if k == ORDER[0]:
            with scope("barrier"):
                pl.semaphore_wait(barrier, NG + NP - 2)
        to_partner(0, k)
        if k != ORDER[0]:
            from_partner(0, last)
        last = k

    for it in range(2):
        if it == 1:
            with scope("w_gar"):
                arrived(0, GAR, NG, gall)
            with scope("chol_right"):
                inv_right = factor_of(total(gall, 0, NG))
        from_partner(it, last)
        with scope("w_prs"):
            view = prs.at[it, pl.ds(1, NY - 1)]
            landed(view, recv_sem.at[it, PRS])
        with scope("pag_send"):
            mine = (part[it, g] + prs[it, 1]) + (prs[it, 2] + prs[it, 3])
            if it == 1:
                mine = product(inv_right, mine)
            panel[it, g] = mine
            own = panel.at[it, g]
            for k in (2, 1, 3):
                send(it, PAG, own, own, gal_peer(2 * chunk(k) + core), near_sem.at[it, NY - k])
            partner = gal_peer(2 * y + other)
            send(it, PAG, own, own, partner, near_sem.at[it, 0])
        with scope("gram_left"):
            gram = twin_gram(mine)
            for d in range(NG):
                kpart[it, d] = gram[d * RB : (d + 1) * RB]
            spread(it, KG, NG, g, gal_peer, lambda t: kpart.at[it, t], kg)
            kg[it, g] = kpart[it, g]

        def send_kz():
            with scope("w_kg"):
                arrived(it, KG, NG, kg)
            kz[it, z] = total(kg, it, NG)
            spread(it, KZ, NZ, z, z_peer, lambda t: kz.at[it, z], kz)

        raw = None

        def relay(k):
            with scope("w_relay"):
                slot = panel.at[it, 2 * chunk(k) + core]
                landed(slot, near_sem.at[it, k])
                send(it, PAG, slot, slot, partner, relay_sem.at[it, k])

        for k in (0, 1, 3, 2):
            block = 2 * chunk(k)
            rows = rows_of(k)
            with scope("w_near"):
                landed(panel.at[it, block + other], near_sem.at[it, 0] if k == 0 else relay_sem.at[it, k])
            with scope("norm"):
                p = jnp.concatenate([panel[it, block], panel[it, block + 1]], axis=1)
                normal[:, rows] = p
            with scope("raw_wide"):
                term = mm3(stacked(p), thi[rows, :], tmid[rows, :], tlo[rows, :], NN)
                raw = term if raw is None else raw + term
            if k == 0:
                for kk in (1, 3, 2):
                    relay(kk)
            if k == 3:
                send_kz()
        with scope("w_send"):
            for i in range(NX):
                for j in range(NZ):
                    wpart[it, i * NZ + j] = raw[j * RB : (j + 1) * RB, i * LB : (i + 1) * LB]
            for k in PIX_ORDER:
                send(it, WRS, wpart.at[it, pix_of(k)], wrs.at[it, pix], pix_peer(k), recv_sem.at[it, WRS])
            wrs[it, pix] = wpart[it, pix]

        with scope("w_kz"):
            arrived(it, KZ, NZ, kz)
        kx[it, x] = total(kz, it, NZ)
        spread(it, KX, NX, x, x_peer, lambda t: kx.at[it, x], kx)

        def finish_k():
            with scope("w_kx"):
                arrived(it, KX, NX, kx)
            kraw[it, g] = total(kx, it, NX)
            spread(it, KAG, NG, g, gal_peer, lambda t: kraw.at[it, g], kraw)

        with scope("w_wrs"):
            arrived(it, WRS, NP, wrs)
        with scope("wag_send"):
            wraw[it, pix] = total(wrs, it, NP)
            own = wraw.at[it, pix]
            for k in PIX_ORDER:
                send(it, WAG, own, own, pix_peer(k), recv_sem.at[it, WAG])
        finish_k()

        with scope("w_kag"):
            arrived(it, KAG, NG, kraw)
        with scope("chol_left"):
            inv_left = inverse_factor(jnp.concatenate([kraw[it, i] for i in range(NG)], axis=0))

        def put_left():
            with scope("left"):
                left = product(inv_left, normal[...])
                l_high, l_low = split(left)
                lstk[0:R, :] = l_high
                lstk[R : 2 * R, :] = l_high
                lstk[2 * R : 3 * R, :] = l_low
                if it == 1:
                    left_ref[...] = left

        if it == 0:
            put_left()
        with scope("w_wag"):
            arrived(it, WAG, NP, wraw)
        with scope("wide"):
            columns = [jnp.concatenate([wraw[it, i * NZ + j] for j in range(NZ)], axis=0) for i in range(NX)]
            wide = product(inv_left, jnp.concatenate(columns, axis=1))
            w_high, w_low = split(wide)
            wstk = jnp.concatenate([w_high, w_low, w_high], axis=0)
            r3 = stacked(wide)
        with scope("gram_right"):
            gram = twin_gram(wide)
            lane = lax.broadcasted_iota(jnp.int32, (R // 2, 128), 1)
            gall[it, g] = jnp.where(lane < R, gram[: R // 2], gram[R // 2 :])
            spread(it, GAR, NG, g, gal_peer, lambda t: gall.at[it, g], gall)
        if it == 1:
            put_left()
        for k in ORDER:
            with scope("update"):
                rows = rows_of(k)
                low = mm(lstk[:, rows], wstk, TN)
                c = dual[rows, :]
                if it == 0:
                    clipped = clip(obs[rows, :] + c - low)
                    dual[rows, :] = clipped
                    panel_chunk(1, k, r3, low - c + (clipped + clipped))
                    to_partner(1, k)
                    if k != ORDER[0]:
                        from_partner(1, last)
                    last = k
                else:
                    v = obs[rows, :] + c - low
                    clipped = clip(v)
                    sparse_out[rows, :] = v - clipped
                    dual_out[rows, :] = MU * clipped

    wide_ref[...] = wide
    with scope("w_gar"):
        arrived(1, GAR, NG, gall)
    gram_ref[...] = total(gall, 1, NG)
    with scope("fin"):
        for it in range(2):
            for kind, n, buf in (
                (PEX, NY + 1, pex), (PRS, NY, prs), (PAG, NG, panel), (WRS, NP, wrs), (WAG, NP, wraw),
                (KG, NG, kg), (KZ, NZ, kz), (KX, NX, kx), (KAG, NG, kraw), (GAR, NG, gall),
            ):
                landed(buf.at[it, pl.ds(0, n - 1)], send_sem.at[it, kind])


def outputs(
    sparse, dual, left, wide, gram, sparse_hbm, dual_hbm, left_hbm, right_hbm, right, sem,
):
    copies = [
        pltpu.make_async_copy(src, dst, sem.at[i])
        for i, (src, dst) in enumerate(((sparse, sparse_hbm), (dual, dual_hbm), (left, left_hbm), (right, right_hbm)))
    ]
    for copy in copies[:3]:
        copy.start()
    right[...] = product(factor_of(gram[...]), wide[...])
    copies[3].start()
    for copy in copies:
        copy.wait()


def per_device(observed, sparse_init, dual_init, right_init):
    hbm = pl.BlockSpec(memory_space=pltpu.HBM)
    vmem = pl.BlockSpec(memory_space=pltpu.VMEM)
    shape = (ROWS, COLS)
    whole = jax.ShapeDtypeStruct(shape, F32)
    left_shape = jax.ShapeDtypeStruct((R, ROWS), F32)
    right_shape = jax.ShapeDtypeStruct((R, COLS), F32)
    state = pl.pallas_call(
        kernel,
        out_shape=(whole, whole, left_shape, right_shape, jax.ShapeDtypeStruct((R // 2, 2 * R), F32)),
        in_specs=[hbm] * 4,
        out_specs=(vmem,) * 5,
        scratch_shapes=[
            pltpu.VMEM((R, COLS), F32),
            pltpu.VMEM(shape, F32),
            pltpu.VMEM(shape, F32),
            pltpu.VMEM(shape, F32),
            pltpu.VMEM(shape, BF16),
            pltpu.VMEM(shape, BF16),
            pltpu.VMEM(shape, BF16),
            pltpu.VMEM((3 * R, ROWS), BF16),
            pltpu.VMEM((2, NG, R, GB), F32),
            pltpu.VMEM((2, NY, R, GB), F32),
            pltpu.VMEM((2, NY, R, GB), F32),
            pltpu.VMEM((2, NG, R, GB), F32),
            pltpu.VMEM((R, ROWS), F32),
            pltpu.VMEM((2, NP, RB, LB), F32),
            pltpu.VMEM((2, NP, RB, LB), F32),
            pltpu.VMEM((2, NP, RB, LB), F32),
            pltpu.VMEM((2, NG, RB, 2 * R), F32),
            pltpu.VMEM((2, NG, RB, 2 * R), F32),
            pltpu.VMEM((2, NZ, RB, 2 * R), F32),
            pltpu.VMEM((2, NX, RB, 2 * R), F32),
            pltpu.VMEM((2, NG, RB, 2 * R), F32),
            pltpu.VMEM((2, NG, R // 2, 2 * R), F32),
            pltpu.SemaphoreType.DMA((4, NY)),
            pltpu.SemaphoreType.DMA((2, 10)),
            pltpu.SemaphoreType.DMA((2, 10)),
            pltpu.SemaphoreType.DMA((2, NY)),
            pltpu.SemaphoreType.DMA((2, NY)),
            pltpu.SemaphoreType.DMA((2, NY)),
        ],
        compiler_params=pltpu.CompilerParams(collective_id=0, has_side_effects=True, vmem_limit_bytes=48 << 20),
        name="pursuit",
    )(*(pltpu.with_memory_space_constraint(a, pltpu.HBM) for a in (observed, sparse_init, dual_init, right_init)))
    return pl.pallas_call(
        outputs,
        out_shape=(whole, whole, left_shape, right_shape),
        in_specs=[vmem] * 5,
        out_specs=(hbm,) * 4,
        scratch_shapes=[
            pltpu.VMEM((R, COLS), F32),
            pltpu.SemaphoreType.DMA((4,)),
        ],
        compiler_params=pltpu.CompilerParams(vmem_limit_bytes=24 << 20),
        name="outputs",
    )(*state)


def solution(mesh):
    return jax.shard_map(
        per_device,
        mesh=mesh,
        in_specs=(P("pix", "gal"), P("pix", "gal"), P("pix", "gal"), P(None, "gal")),
        out_specs=(P("pix", "gal"), P("pix", "gal"), P(None, "pix"), P(None, "gal")),
        check_vma=False,
    )
```
